32 devices in a mesh: rep: 2 (over y), shard: 16 (over z, x, core).
Axes of the slice: x: 2, y: 2, z: 4, core: 2. Of those that a mesh axis runs over, the one named last changes fastest.
Arguments:
- tokens: bfloat16 [32768, 1024], P(('rep', 'shard')), may hold values from -6 to 6
- teacher: bfloat16 [32768, 1024], P(('rep', 'shard')), may hold values from -6 to 6
- valid: int32 [32768], P(('rep', 'shard')), may hold values from 0 to 1
- segments: int32 [32, 1024], P(('rep', 'shard')), may hold values from 0 to 7, as said below
- positions: int32 [32, 1024], P(('rep', 'shard')), may hold values from 0 to 2046, as said below
- w_qkv: bfloat16 [1024, 3072], P('shard'), may hold values from -0.1875 to 0.1875
- w_out: bfloat16 [1024, 1024], P('shard'), may hold values from -0.1875 to 0.1875
- w_upgate: bfloat16 [1024, 8192], P('shard'), may hold values from -0.1875 to 0.1875
- w_down: bfloat16 [4096, 1024], P('shard'), may hold values from -0.09375 to 0.09375
- s_qk: bfloat16 [1024], P('shard'), may hold values from 0.69921875 to 1.5
- alpha_attn: bfloat16 [1024], P('shard'), may hold values from 0.049804688 to 0.5
- s_up: bfloat16 [4096], P('shard'), may hold values from 0.5 to 1.5
- s_gate: bfloat16 [4096], P('shard'), may hold values from 0.5 to 2
- alpha_mlp: bfloat16 [1024], P('shard'), may hold values from 0.049804688 to 0.5
Outputs:
- output: bfloat16 [32768, 1024], P(('rep', 'shard'))
- loss: float32 [], replicated
- grad_x: float32 [32768, 1024], P(('rep', 'shard'))
- grad_w_qkv: float32 [1024, 3072], P('shard')
- grad_w_out: float32 [1024, 1024], P('shard')
- grad_w_upgate: float32 [1024, 8192], P('shard')
- grad_w_down: float32 [4096, 1024], P('shard')
- grad_s_qk: float32 [1024], P('shard')
- grad_alpha_attn: float32 [1024], P('shard')
- grad_s_up: float32 [4096], P('shard')
- grad_s_gate: float32 [4096], P('shard')
- grad_alpha_mlp: float32 [1024], P('shard')
The draws below stay inside these ranges and needn't reach their ends.
Inputs may be any that keep to these rules, and one draw needn't show every extreme that they name: `segments`: in each sequence document numbers start at 0 at the first token, never fall, and every number up to 7 appears. Within a document positions rise by 1 or 2 from token to token; in each sequence the first document starts at position 0 and the last token has position 2046.
All inputs are finite; a program needn't handle non-finite values.
Results may differ from the reference program's by a relative error of at most 0.02.
Values may be sent and summed in bfloat16 or wider, within the bound.
No kernel may reach another device: no remote copies, remote signals or barrier semaphores. Data moves between devices by JAX's collectives and lax.ppermute only.
A program may use at most 384 MiB of HBM per device.

```python
import math
import jax
import jax.numpy as jnp
from jax import lax

D = 1024
HEADS = 16
FF = 4096
HEAD_DIM = 64
SEQ_LEN = 1024
DOCS = 8
NSEQ = 32
TOKENS = 32768


def doc_layout(key):
    score_key = jax.random.fold_in(key, 11)
    stride_key = jax.random.fold_in(key, 13)
    places = jnp.arange(1, SEQ_LEN, dtype=jnp.int32)
    noise = jax.random.randint(score_key, (NSEQ, SEQ_LEN - 1), 0, 1 << 20)
    scores = noise * SEQ_LEN + places[None, :]
    chosen = lax.top_k(scores, DOCS - 1)[0] % SEQ_LEN
    every = jnp.arange(SEQ_LEN, dtype=jnp.int32)
    cuts = jnp.sum((every[None, :, None] == chosen[:, None, :]).astype(jnp.int32), axis=-1)
    segments = jnp.cumsum(cuts, axis=1)
    firsts = jnp.maximum(cuts, (every == 0).astype(jnp.int32)[None, :])
    strides = jax.random.randint(stride_key, (NSEQ, SEQ_LEN), 1, 3)
    before = jnp.cumsum(strides, axis=1) - strides
    base = lax.cummax(before * firsts, axis=1)
    local = before - base
    last_doc = (segments == DOCS - 1).astype(jnp.int32)
    lift = 2 * SEQ_LEN - 2 - local[:, -1:]
    placed = local + last_doc * lift
    return (segments.astype(jnp.int32), placed.astype(jnp.int32))


def draw_segments(key, part):
    return doc_layout(jax.random.fold_in(key, 5))[0]


def draw_positions(key, part):
    return doc_layout(jax.random.fold_in(key, 5))[1]


def draw_valid(key, part):
    index = jnp.arange(TOKENS, dtype=jnp.int32)
    threshold = 300 + 600 * index // TOKENS
    rolls = jax.random.randint(jax.random.fold_in(key, 3), (TOKENS,), 0, 1000)
    return (rolls < threshold).astype(jnp.int32)


def level_of(key, dims, cuts, smallest, high):
    level, own = 1.0, jax.random.fold_in(key, 6)
    for axis_at, blocks in cuts:
        heights = jnp.exp(jax.random.uniform(jax.random.fold_in(own, axis_at), (blocks,), jnp.float32, smallest / len(cuts), high / len(cuts)))
        level = level * jnp.repeat(heights, dims[axis_at] // blocks).reshape([-1 if axis == axis_at else 1 for axis in range(len(dims))])
    return level


def scatter_about(stream_key, shape, deviation, reach, pieces=(), kind=jnp.bfloat16):
    drawn = jax.random.normal(stream_key, shape, jnp.float32) * deviation
    if len(pieces) > 0:
        drawn = level_of(stream_key, shape, pieces, -0.22, 0.18) * drawn
    return jnp.clip(drawn, min=-reach, max=reach).astype(kind)


def setup_inputs(seed: int = 0) -> dict:
    keys = jax.random.split(jax.random.key(seed), 15)
    return {
        "tokens": scatter_about(keys[0], (TOKENS, D), 1.0, 6.0, ((0, 32),)),
        "teacher": scatter_about(keys[1], (TOKENS, D), 1.0, 6.0, ((0, 32),)),
        "valid": draw_valid(jax.random.fold_in(keys[14], 71), 0),
        "segments": draw_segments(jax.random.fold_in(keys[14], 71), 0),
        "positions": draw_positions(jax.random.fold_in(keys[14], 71), 0),
        "w_qkv": scatter_about(keys[5], (D, 3 * D), D ** -0.5, 0.1875, ((0, 16),)),
        "w_out": scatter_about(keys[6], (D, D), D ** -0.5, 0.1875, ((0, 16),)),
        "w_upgate": scatter_about(keys[7], (D, 2 * FF), D ** -0.5, 0.1875, ((0, 16),)),
        "w_down": scatter_about(keys[8], (FF, D), FF ** -0.5, 0.09375, ((0, 16),)),
        "s_qk": jnp.clip(0.69921875 + 0.80078125 * jax.random.uniform(keys[9], (D,), jnp.float32) ** level_of(keys[9], (D,), ((0, 16),), -0.2, 0.2), 0.69921875, 1.5).astype(jnp.bfloat16),
        "alpha_attn": jnp.clip(jnp.exp(math.log(0.5) - 2.306499 * jax.random.uniform(keys[10], (D,), jnp.float32) ** level_of(keys[10], (D,), ((0, 16),), -0.2, 0.2)), 0.049804688, 0.5).astype(jnp.bfloat16),
        "s_up": jnp.clip(0.5 + 1.0 * jax.random.uniform(keys[11], (FF,), jnp.float32) ** level_of(keys[11], (FF,), ((0, 16),), -0.2, 0.2), 0.5, 1.5).astype(jnp.bfloat16),
        "s_gate": jnp.clip(0.5 + 1.5 * jax.random.uniform(keys[12], (FF,), jnp.float32) ** level_of(keys[12], (FF,), ((0, 16),), -0.2, 0.2), 0.5, 2.0).astype(jnp.bfloat16),
        "alpha_mlp": jnp.clip(jnp.exp(math.log(0.5) - 2.306499 * jax.random.uniform(keys[13], (D,), jnp.float32) ** level_of(keys[13], (D,), ((0, 16),), -0.2, 0.2)), 0.049804688, 0.5).astype(jnp.bfloat16),
    }


EPS = 1e-06
HIGH = lax.Precision.HIGHEST

@jax.custom_vjp
def low(v):
    return lax.optimization_barrier(v.astype(jnp.bfloat16)).astype(jnp.float32)

@jax.custom_vjp
def low_back(v):
    return v

def low_keep(v):
    return (low(v), None)

def low_pass(kept, grad):
    return (grad,)

def back_keep(v):
    return (v, None)

def back_low(kept, grad):
    return (low(grad),)
low.defvjp(low_keep, low_pass)
low_back.defvjp(back_keep, back_low)

def matmul(left, right):
    return jnp.dot(left, right, precision=HIGH, preferred_element_type=jnp.float32)

def row_norm(value):
    return value * lax.rsqrt(lax.optimization_barrier(jnp.mean(value * value, axis=-1, keepdims=True)) + EPS)

def rotate(value, cosine, sine):
    half = value.shape[-1] // 2
    first = value[..., :half]
    second = value[..., half:]
    return jnp.concatenate([first * cosine - second * sine, second * cosine + first * sine], axis=-1)

def rotary_tables(positions, head_dim):
    half = head_dim // 2
    freq = jnp.power(10000.0, -2.0 * jnp.arange(half, dtype=jnp.float32) / head_dim)
    angle = positions.astype(jnp.float32)[..., None] * freq
    return (jnp.cos(angle)[..., None, :], jnp.sin(angle)[..., None, :])

def attend(items):
    query, key, value, seg = items
    raw = jnp.einsum('qhd,khd->hqk', query, key, precision=HIGH) * math.sqrt(HEAD_DIM)
    raw = low_back(raw)
    spots = jnp.arange(SEQ_LEN)
    allowed = (seg[:, None] == seg[None, :]) & (spots[:, None] >= spots[None, :])
    masked = jnp.where(allowed[None], raw, -jnp.inf)
    peak = lax.optimization_barrier(jnp.max(masked, axis=-1, keepdims=True))
    expo = jnp.exp(masked - peak)
    probs = expo / lax.optimization_barrier(jnp.sum(expo, axis=-1, keepdims=True))
    return jnp.einsum('hqk,khd->qhd', low(probs), value, precision=HIGH)

def forward(x, params, teacher, mask_f, seg, pos):
    w_qkv, w_out, w_ug, w_down, s_qk, a_attn, s_up, s_gate, a_mlp = params
    rows = x.shape[0]
    count_seq = seg.shape[0]
    shape = (count_seq, SEQ_LEN, HEADS, HEAD_DIM)
    qkv = low(low_back(matmul(x, w_qkv)))
    cosine, sine = rotary_tables(pos, HEAD_DIM)
    q_rot = rotate(qkv[:, :D].reshape(shape), cosine, sine)
    k_rot = rotate(qkv[:, D:2 * D].reshape(shape), cosine, sine)
    values = qkv[:, 2 * D:].reshape(shape)
    scale_qk = s_qk.reshape(HEADS, HEAD_DIM)
    q_unit = q_rot * lax.rsqrt(lax.optimization_barrier(jnp.sum(q_rot * q_rot, axis=-1, keepdims=True)) + EPS)
    k_unit = k_rot * lax.rsqrt(lax.optimization_barrier(jnp.sum(k_rot * k_rot, axis=-1, keepdims=True)) + EPS)
    q_two = low(q_unit * scale_qk)
    k_two = low(k_unit * scale_qk)
    attended = lax.map(jax.checkpoint(attend), (q_two, k_two, values, seg))
    attended = low(low_back(attended.reshape(rows, D)))
    branch_a = low_back(matmul(attended, w_out))
    h_one = row_norm(x + a_attn * (row_norm(branch_a) - x))
    up_gate = low_back(matmul(low(h_one), w_ug))
    up = up_gate[:, :FF] * s_up
    gate = up_gate[:, FF:] * s_gate
    hidden = low(up * jax.nn.silu(gate))
    branch_m = low_back(matmul(hidden, w_down))
    h_two = row_norm(h_one + a_mlp * (row_norm(branch_m) - h_one))
    diff = h_two - teacher
    return (h_two, jnp.sum(mask_f[:, None] * diff * diff))

def reference(tokens, teacher, valid, segments, positions, w_qkv, w_out, w_upgate, w_down, s_qk, alpha_attn, s_up, s_gate, alpha_mlp):
    params = tuple((p.astype(jnp.float32) for p in (w_qkv, w_out, w_upgate, w_down, s_qk, alpha_attn, s_up, s_gate, alpha_mlp)))
    mask_f = valid.astype(jnp.float32)
    count = jnp.maximum(jnp.sum(mask_f), 1.0)
    scale = TOKENS / count
    group = max(1, 4096 // SEQ_LEN)
    while NSEQ % group:
        group -= 1
    turns = NSEQ // group
    rows = group * SEQ_LEN
    inputs = (tokens.astype(jnp.float32).reshape(turns, rows, D), teacher.astype(jnp.float32).reshape(turns, rows, D), mask_f.reshape(turns, rows), segments.reshape(turns, group, SEQ_LEN), positions.reshape(turns, group, SEQ_LEN))

    def step(acc, items):
        x_part, t_part, m_part, s_part, p_part = items

        def closed(x_value, *weights):
            return forward(x_value, weights, t_part, m_part, s_part, p_part)
        (h_two, lsum), pull = jax.vjp(closed, x_part, *params)
        grads = pull((jnp.zeros_like(h_two), scale))
        acc = tuple((a + g for a, g in zip(acc, grads[1:])))
        return (acc, (h_two.astype(jnp.bfloat16), lsum, grads[0]))
    init = tuple((jnp.zeros_like(p) for p in params))
    acc, (outputs, lsums, grad_parts) = lax.scan(step, init, inputs)
    loss = jnp.sum(lsums) / count
    return (outputs.reshape(TOKENS, D), loss, grad_parts.reshape(TOKENS, D), acc[0], acc[1], acc[2], acc[3], acc[4], acc[5], acc[6], acc[7], acc[8])
```

```python
from functools import partial
import math

import jax
import jax.numpy as jnp
from jax import lax
from jax.experimental import pallas as pl
from jax.experimental.pallas import tpu as pltpu
from jax.sharding import PartitionSpec as P

EPS = 1e-06
AXES = ("rep", "shard")
NZ = 4
NC = 2


class Place:
    def __init__(self):
        self.reps = lax.axis_size("rep")
        self.shards = lax.axis_size("shard")
        self.nx = self.shards // (NZ * NC)
        self.pairs = self.reps % 2 == 0
        rep = lax.axis_index("rep")
        shard = lax.axis_index("shard")
        self.rep = rep
        self.shard = shard
        self.y = rep % 2
        self.core = shard % NC
        self.x = (shard // NC) % self.nx
        self.z = shard // (NC * self.nx)

    def moves(self, step):
        pairs = []
        for rep in range(self.reps):
            for z in range(NZ):
                for x in range(self.nx):
                    for core in range(NC):
                        to_rep, to_z, to_x, to_core = step(rep, z, x, core)
                        pairs.append(
                            (
                                rep * self.shards + (z * self.nx + x) * NC + core,
                                to_rep * self.shards + (to_z * self.nx + to_x) * NC + to_core,
                            )
                        )
        return pairs

    def near_z(self, value):
        return lax.ppermute(value, AXES, self.moves(lambda r, z, x, c: (r, z ^ 1, x, c)))

    def far_z(self, value):
        return lax.ppermute(value, AXES, self.moves(lambda r, z, x, c: (r, z ^ (2 + r % 2), x, c)))

    def along_x(self, value, j):
        return lax.ppermute(value, AXES, self.moves(lambda r, z, x, c: (r, z, x ^ j, c)))

    def along_y(self, value):
        return lax.ppermute(value, AXES, self.moves(lambda r, z, x, c: (r ^ 1, z, x, c)))

    def other_core(self, value):
        return lax.ppermute(value, AXES, self.moves(lambda r, z, x, c: (r, z, x, c ^ 1)))

    def flat(self, value, bit):
        count = self.reps * self.shards
        return lax.ppermute(value, AXES, [(i, i ^ bit) for i in range(count)])

    def slot(self, k, j):
        return (self.z ^ k) * self.nx + (self.x ^ j)


def tie(*values):
    return lax.optimization_barrier(values)


def place_kernel(count, slots, *refs):
    pieces, out = refs[:-1], refs[-1]
    for i in range(count):
        rows = pieces[i].shape[0]
        at = pl.multiple_of(slots[i] * rows, rows)
        out[pl.ds(at, rows), :] = pieces[i][...]


def assemble(pieces, slots, rows_out):
    cols = pieces[0].shape[1]
    size = rows_out * cols * pieces[0].dtype.itemsize
    return pl.pallas_call(
        partial(place_kernel, len(pieces)),
        out_shape=jax.ShapeDtypeStruct((rows_out, cols), pieces[0].dtype),
        in_specs=[pl.BlockSpec(memory_space=pltpu.SMEM)]
        + [pl.BlockSpec(memory_space=pltpu.VMEM)] * len(pieces),
        out_specs=pl.BlockSpec(memory_space=pltpu.VMEM),
        compiler_params=pltpu.CompilerParams(vmem_limit_bytes=2 * size + (4 << 20)),
        cost_estimate=pl.CostEstimate(flops=0, bytes_accessed=2 * size, transcendentals=0),
    )(slots, *pieces)


def weave_kernel(core, half, other, out, sems):
    at = core[0]
    first = pltpu.make_async_copy(half, out.at[:, at], sems.at[0])
    second = pltpu.make_async_copy(other, out.at[:, 1 - at], sems.at[1])
    first.start()
    second.start()
    first.wait()
    second.wait()


def weave(half, other, core, groups):
    rows, cols = half.shape
    each = rows // groups
    size = rows * cols * half.dtype.itemsize
    shape = (groups, each, cols)
    full = pl.pallas_call(
        weave_kernel,
        out_shape=jax.ShapeDtypeStruct((groups, 2, each, cols), half.dtype),
        in_specs=[
            pl.BlockSpec(memory_space=pltpu.SMEM),
            pl.BlockSpec(memory_space=pltpu.VMEM),
            pl.BlockSpec(memory_space=pltpu.VMEM),
        ],
        out_specs=pl.BlockSpec(memory_space=pl.ANY),
        scratch_shapes=[pltpu.SemaphoreType.DMA((2,))],
        compiler_params=pltpu.CompilerParams(vmem_limit_bytes=2 * size + (4 << 20)),
        cost_estimate=pl.CostEstimate(flops=0, bytes_accessed=4 * size, transcendentals=0),
    )(core, half.reshape(shape), other.reshape(shape))
    return full.reshape(2 * rows, cols)


class Gather:
    def __init__(self, at, chunks):
        self.at = at
        self.ready = list(chunks)
        self.near, self.far, self.over_x, self.over_y = {}, {}, {}, {}
        self.own, self.other = {}, {}
        self.groups = NZ * at.nx
        self.core = at.core.reshape(1).astype(jnp.int32)

    def tick(self, tick, gate):
        at = self.at
        count = len(self.ready)
        offsets = range(1, at.nx)
        y = at.y
        ended = []
        if tick < count:
            piece = after(self.ready[tick], gate)
            self.ready[tick] = piece
            self.near[tick] = at.near_z(piece)
            self.far[tick] = at.far_z(piece)
            ended += [self.near[tick], self.far[tick]]
        i = tick - 1
        if 0 <= i < count:
            piece = self.ready[i]
            rows = piece.shape[0]
            half = lax.dynamic_slice_in_dim(piece, y * (rows // 2), rows // 2, axis=0)
            send = after(jnp.concatenate([half, self.near[i], self.far[i]], axis=0), gate)
            self.over_x[i] = [at.along_x(send, j) for j in offsets]
            ended += self.over_x[i]
        i = tick - 2
        if 0 <= i < count:
            rows = self.ready[i].shape[0]
            sends = [self.far[i]]
            for got in self.over_x[i]:
                sends += [got[: rows // 2], got[rows // 2 + rows :]]
            self.over_y[i] = at.along_y(after(jnp.concatenate(sends, axis=0), gate))
            ended += [self.over_y[i]]
        i = tick - 3
        if 0 <= i < count:
            rows = self.ready[i].shape[0]
            half = rows // 2
            got = self.over_y[i]
            pieces = [self.ready[i], self.near[i], self.far[i], got[:rows]]
            slots = [at.slot(0, 0), at.slot(1, 0), at.slot(2 + y, 0), at.slot(3 - y, 0)]
            place = rows
            for mine, j in zip(self.over_x[i], offsets):
                pieces += [mine[:half], mine[half : half + rows], mine[half + rows :]]
                slots += [at.slot(0, j) * 2 + y, at.slot(1, j), at.slot(2 + y, j)]
                pieces += [got[place : place + half], got[place + half : place + half + rows]]
                slots += [at.slot(0, j) * 2 + (1 - y), at.slot(3 - y, j)]
                place += half + rows
            self.own[i] = assemble(pieces, jnp.stack(slots).astype(jnp.int32), self.groups * rows)
            self.other[i] = at.other_core(after(self.own[i], gate))
            ended += [self.other[i]]
        return ended

    def full(self, i):
        return weave(self.own[i], self.other[i], self.core, self.groups)


def after(value, gate):
    return tie(value, *gate)[0] if gate else value


class Reduce:
    def __init__(self, at, send, keep):
        self.at = at
        self.send = send
        self.keep = keep
        self.rows = keep.shape[0] // (NZ * at.nx)
        self.stage = 0

    def add(self, places, extras=()):
        slots = [self.at.slot(k, j) for k, j in places]
        return add_slots(self.keep, self.got, self.rows, slots, extras)

    def step(self, gate):
        at = self.at
        offsets = range(1, at.nx)
        y = at.y
        stage = self.stage
        self.stage += 1
        if stage == 0:
            self.got = at.other_core(after(self.send, gate))
            return [self.got]
        if stage == 1:
            send = self.add([(3 - y, j) for j in range(at.nx)])
            self.got_y = at.along_y(after(send, gate))
            return [self.got_y]
        if stage == 2:
            self.got_x = []
            for j in offsets:
                send = self.add([(0, j), (1, j), (2 + y, j)], [(self.got_y, [None, None, j])])
                self.got_x.append(at.along_x(after(send, gate), j))
            return self.got_x
        if stage == 3:
            near = self.add([(1, 0)], [(g, [1]) for g in self.got_x])
            far = self.add([(2 + y, 0)], [(self.got_y, [0])] + [(g, [2]) for g in self.got_x])
            self.near = at.near_z(after(near, gate))
            self.far = at.far_z(after(far, gate))
            return [self.near, self.far]
        if stage == 4:
            terms = [(self.near, [0]), (self.far, [0])] + [(g, [0]) for g in self.got_x]
            self.mine = after(self.add([(0, 0)], terms), gate)
            self.last = at.along_y(self.mine)
            return [self.last]
        return []

    def total(self):
        return over_copies(self.at, self.mine.astype(jnp.float32) + self.last.astype(jnp.float32), 2)


def over_copies(at, total, bit):
    while bit < at.reps:
        total = total + at.flat(total.astype(jnp.bfloat16), bit * at.shards).astype(jnp.float32)
        bit *= 2
    return total


def sum_everywhere(at, value):
    bit = 1
    while bit < at.reps * at.shards:
        value = value + at.flat(value, bit)
        bit *= 2
    return value


def gather_vectors(at, vectors):
    sizes = [v.shape[0] for v in vectors]
    flat = jnp.concatenate(vectors)
    length = -(-flat.shape[0] // 128) * 128
    flat = jnp.pad(flat, (0, length - flat.shape[0])).reshape(1, length)
    bit = 1
    while bit < at.shards:
        other = at.flat(flat, bit)
        low = (at.shard // bit) % 2 == 0
        flat = jnp.where(
            low, jnp.concatenate([flat, other], axis=0), jnp.concatenate([other, flat], axis=0)
        )
        bit *= 2
    out = []
    start = 0
    for size in sizes:
        out.append(flat[:, start : start + size].reshape(-1))
        start += size
    return out


LOG2E = 1.4426950408889634
HEAD = 64
PAIR = 128
ROWS_Q = 256
ROWS_K = 256


def lanes_of(shape):
    return lax.broadcasted_iota(jnp.int32, shape, len(shape) - 1)


def half_turn(value):
    low = lanes_of(value.shape) % HEAD < HEAD // 2
    return jnp.where(low, pltpu.roll(value, PAIR - HEAD // 2, 1), pltpu.roll(value, HEAD // 2, 1))


def swap_matrix():
    left = lax.broadcasted_iota(jnp.int32, (PAIR, PAIR), 0)
    right = lax.broadcasted_iota(jnp.int32, (PAIR, PAIR), 1)
    return (left == (right ^ (HEAD // 2))).astype(jnp.bfloat16)


def two_parts(value):
    high = value.astype(jnp.bfloat16)
    return high, (value - high.astype(jnp.float32)).astype(jnp.bfloat16)


def head_sum(value):
    left = lax.broadcasted_iota(jnp.int32, (2 * PAIR, PAIR), 0) // HEAD % 2
    right = lax.broadcasted_iota(jnp.int32, (2 * PAIR, PAIR), 1) // HEAD
    same = (left == right).astype(jnp.bfloat16)
    parts = jnp.concatenate(two_parts(value), axis=1)
    return jnp.dot(parts, same, preferred_element_type=jnp.float32)


def turned(raw, cosine, sine):
    swapped = jnp.dot(raw, swap_matrix(), preferred_element_type=jnp.float32)
    rot = raw.astype(jnp.float32) * cosine + swapped * sine
    factor = lax.rsqrt(head_sum(rot * rot) + EPS)
    return rot * factor, factor


def only(value, head):
    mine = lanes_of(value.shape) // HEAD == head
    return jnp.where(mine, value, jnp.zeros_like(value))


def dot_last(a, b):
    return lax.dot_general(a, b, (((1,), (1,)), ((), ())), preferred_element_type=jnp.float32)


def dot_first(a, b):
    return lax.dot_general(a, b, (((0,), (0,)), ((), ())), preferred_element_type=jnp.float32)


FAR = -16384.0


def spare_lane(shape, head):
    return lanes_of(shape) - (1 - head) * HEAD


def query_lanes(value, head, segs):
    spare = spare_lane(value.shape, head)
    own = lanes_of(value.shape) // HEAD == head
    marks = (spare >= 0) & (spare < 8) & (spare != segs)
    return jnp.where(own, value.astype(jnp.float32), jnp.where(marks, FAR, 0.0)).astype(value.dtype)


def key_lanes(value, head, segs):
    spare = spare_lane(value.shape, head)
    own = lanes_of(value.shape) // HEAD == head
    return jnp.where(own, value.astype(jnp.float32), (spare == segs).astype(jnp.float32)).astype(value.dtype)


def attend_kernel(temper, q_ref, k_ref, v_ref, cos_ref, sin_ref, scale_ref, seg_ref, out_ref, lse_ref,
                  q_sc, k_sc, v_sc, sum_sc):
    length = q_ref.shape[0]
    bf16 = jnp.bfloat16
    f32 = jnp.float32
    scale = scale_ref[...]
    cosine = cos_ref[...]
    sine = sin_ref[...]
    segs = seg_ref[...]
    q2 = (turned(q_ref[...], cosine, sine)[0] * scale).astype(bf16)
    k2 = (turned(k_ref[...], cosine, sine)[0] * scale).astype(bf16)
    v = v_ref[...]
    ones = jnp.ones_like(v)
    for head in range(2):
        q_sc[head] = query_lanes(q2, head, segs)
        k_sc[head] = key_lanes(k2, head, segs)
        v_sc[head, :, :PAIR] = only(v, head)
        v_sc[head, :, PAIR:] = only(ones, head)
    factor = temper * LOG2E
    size = min(ROWS_Q, length)
    blocks = length // size
    causal = lax.broadcasted_iota(jnp.int32, (size, size), 0) >= lax.broadcasted_iota(
        jnp.int32, (size, size), 1
    )
    for block in range(blocks):
        at = block * size
        for head in range(2):
            keys = k_sc[head, at : at + size, :]
            raw = dot_last(q_sc[head, at:, :], keys)
            expo = causal_top(jnp.exp2(raw * factor), causal).astype(bf16)
            part = jnp.dot(expo, v_sc[head, at : at + size, :], preferred_element_type=f32)
            if block == 0 and head == 0:
                sum_sc[...] = part
            else:
                sum_sc[at:, :] += part
    mass = sum_sc[:, PAIR:]
    out_ref[...] = (sum_sc[:, :PAIR] / mass).astype(bf16)
    lse_ref[...] = jnp.log2(mass)


def causal_top(value, causal):
    size = causal.shape[0]
    edge = jnp.where(causal, value[:size, :], 0.0)
    if value.shape[0] == size:
        return edge
    return jnp.concatenate([edge, value[size:, :]], axis=0)


def causal_bottom(value, causal):
    size = causal.shape[0]
    edge = jnp.where(causal, value[-size:, :], 0.0)
    if value.shape[0] == size:
        return edge
    return jnp.concatenate([value[:-size, :], edge], axis=0)


def pair_spec(length, offset):
    return pl.BlockSpec((length, PAIR), lambda p: (0, p + offset))


def attention(qkv, cosine, sine, scale, segs, offset):
    length, width = qkv.shape[0], qkv.shape[1] // 3
    pairs = width // PAIR
    whole = pl.BlockSpec((length, PAIR), lambda p: (0, 0))
    column = pl.BlockSpec((length, 1), lambda p: (0, 0))
    return pl.pallas_call(
        partial(attend_kernel, math.sqrt(HEAD)),
        grid=(pairs,),
        in_specs=[
            pair_spec(length, 0), pair_spec(length, pairs), pair_spec(length, 2 * pairs),
            whole, whole, pl.BlockSpec((1, PAIR), lambda p: (0, p + offset // PAIR)), column,
        ],
        out_specs=[pair_spec(length, 0), pair_spec(length, 0)],
        scratch_shapes=[
            pltpu.VMEM((2, length, PAIR), jnp.bfloat16),
            pltpu.VMEM((2, length, PAIR), jnp.bfloat16),
            pltpu.VMEM((2, length, 2 * PAIR), jnp.bfloat16),
            pltpu.VMEM((length, 2 * PAIR), jnp.float32),
        ],
        out_shape=[
            jax.ShapeDtypeStruct((length, width), jnp.bfloat16),
            jax.ShapeDtypeStruct((length, width), jnp.float32),
        ],
        compiler_params=pltpu.CompilerParams(vmem_limit_bytes=40 << 20),
        cost_estimate=pl.CostEstimate(
            flops=16 * length * length * width // 2, bytes_accessed=8 * length * width,
            transcendentals=length * length * width // HEAD // 2,
        ),
        name="attend",
    )(qkv, qkv, qkv, cosine, sine, scale, segs)


def three_parts(value):
    high = value.astype(jnp.bfloat16).astype(jnp.float32)
    rest = value - high
    mid = rest.astype(jnp.bfloat16).astype(jnp.float32)
    return high, mid, rest - mid


def attend_back_kernel(temper, q_ref, k_ref, v_ref, o_ref, g_ref, cos_ref, sin_ref, scale_ref, seg_ref, lse_ref,
                       g3_ref, gs_ref, q_sc, k_sc, v_sc, g_sc, dq_sc, dk_sc, dv_sc):
    length = q_ref.shape[0]
    bf16 = jnp.bfloat16
    f32 = jnp.float32
    scale = scale_ref[...]
    cosine = cos_ref[...]
    sine = sin_ref[...]
    segs = seg_ref[...]
    qn, q_factor = turned(q_ref[...], cosine, sine)
    kn, k_factor = turned(k_ref[...], cosine, sine)
    q2 = (qn * scale).astype(bf16)
    k2 = (kn * scale).astype(bf16)
    v = v_ref[...]
    grad = g_ref[...]
    spread = head_sum(grad.astype(f32) * o_ref[...].astype(f32))
    factor = temper * LOG2E
    lanes = lanes_of((length, PAIR))
    for head in range(2):
        spare = spare_lane((length, PAIR), head)
        own = lanes // HEAD == head
        parts = three_parts(lse_ref[:, head * HEAD : head * HEAD + 1] * (-1.0 / factor))
        marks = jnp.where((spare >= 0) & (spare < 8) & (spare != segs), FAR, 0.0)
        for n in range(3):
            marks = jnp.where(spare == 8 + n, parts[n], marks)
        q_sc[head] = jnp.where(own, q2.astype(f32), marks).astype(bf16)
        k_sc[head] = jnp.where(
            own, k2.astype(f32), ((spare == segs) | ((spare >= 8) & (spare < 11))).astype(f32)
        ).astype(bf16)
        parts = three_parts(-spread[:, head * HEAD : head * HEAD + 1])
        marks = jnp.zeros((length, PAIR), f32)
        for n in range(3):
            marks = jnp.where(spare == n, parts[n], marks)
        g_sc[head] = jnp.where(own, grad.astype(f32), marks).astype(bf16)
        v_sc[head] = jnp.where(own, v.astype(f32), ((spare >= 0) & (spare < 3)).astype(f32)).astype(bf16)
    size = min(ROWS_K, length)
    causal = lax.broadcasted_iota(jnp.int32, (size, size), 0) <= lax.broadcasted_iota(
        jnp.int32, (size, size), 1
    )
    blocks = length // size
    lanes = lanes_of((size, PAIR)) // HEAD
    for block in range(blocks - 1, -1, -1):
        at = block * size
        end = at + size
        dqs = []
        for head in range(2):
            queries = q_sc[head, at:end, :]
            grads = g_sc[head, at:end, :]
            keys = k_sc[head, :end, :]
            probs = causal_bottom(jnp.exp2(dot_last(keys, queries) * factor), causal)
            ds = (probs * dot_last(v_sc[head, :end, :], grads)).astype(bf16)
            dv = jnp.dot(probs.astype(bf16), grads, preferred_element_type=f32)
            dk = jnp.dot(ds, queries, preferred_element_type=f32)
            dqs.append(dot_first(ds, keys))
            if block == blocks - 1:
                dv_sc[head] = dv
                dk_sc[head] = dk
            else:
                dv_sc[head, :end, :] += dv
                dk_sc[head, :end, :] += dk
        dq_sc[at:end, :] = jnp.where(lanes == 0, dqs[0], dqs[1])
    lanes = lanes_of((length, PAIR)) // HEAD
    g3_ref[2] = jnp.where(lanes == 0, dv_sc[0], dv_sc[1]).astype(bf16)
    dq = dq_sc[...] * temper
    dk = jnp.where(lanes == 0, dk_sc[0], dk_sc[1]) * temper
    gs_ref[0] = jnp.broadcast_to(jnp.sum(dq * qn + dk * kn, axis=0, keepdims=True), (8, PAIR))

    def unturn(grad, unit, unit_factor):
        grad = grad * scale
        rot = unit_factor * (grad - unit * head_sum(grad * unit))
        return (rot * cosine + half_turn(rot * sine)).astype(bf16)

    g3_ref[0] = unturn(dq, qn, q_factor)
    g3_ref[1] = unturn(dk, kn, k_factor)


def attention_back(qkv, out, grad, lse, cosine, sine, scale, segs, offset, first, pairs):
    length, width = qkv.shape[0], qkv.shape[1] // 3
    every = width // PAIR
    base = offset // PAIR
    whole = pl.BlockSpec((length, PAIR), lambda p: (0, 0))
    column = pl.BlockSpec((length, 1), lambda p: (0, 0))
    return pl.pallas_call(
        partial(attend_back_kernel, math.sqrt(HEAD)),
        grid=(pairs,),
        in_specs=[
            pair_spec(length, first), pair_spec(length, first + every), pair_spec(length, first + 2 * every),
            pair_spec(length, first), pair_spec(length, first + base),
            whole, whole, pl.BlockSpec((1, PAIR), lambda p: (0, p + first + base)), column, pair_spec(length, first),
        ],
        out_specs=[
            pl.BlockSpec((3, length, PAIR), lambda p: (0, 0, p)),
            pl.BlockSpec((1, 8, PAIR), lambda p: (p, 0, 0)),
        ],
        scratch_shapes=[pltpu.VMEM((2, length, PAIR), jnp.bfloat16)] * 4
        + [pltpu.VMEM((length, PAIR), jnp.float32)]
        + [pltpu.VMEM((2, length, PAIR), jnp.float32)] * 2,
        out_shape=[
            jax.ShapeDtypeStruct((3, length, pairs * PAIR), jnp.bfloat16),
            jax.ShapeDtypeStruct((pairs, 8, PAIR), jnp.float32),
        ],
        compiler_params=pltpu.CompilerParams(vmem_limit_bytes=48 << 20),
        cost_estimate=pl.CostEstimate(
            flops=60 * length * length * pairs * PAIR, bytes_accessed=18 * length * pairs * PAIR,
            transcendentals=length * length * pairs * 2,
        ),
        name="attend_back",
    )(qkv, qkv, qkv, out, grad, cosine, sine, scale, segs, lse)


def rotary_wide(positions):
    half = HEAD // 2
    freq = jnp.power(10000.0, -2.0 * jnp.arange(half, dtype=jnp.float32) / HEAD)
    angle = positions.astype(jnp.float32)[:, None] * freq
    cosine = jnp.cos(angle)
    sine = jnp.sin(angle)
    return (
        jnp.concatenate([cosine] * 4, axis=1),
        jnp.concatenate([-sine, sine, -sine, sine], axis=1),
    )


def mean_last(value):
    return jnp.mean(value, axis=-1, keepdims=True)


def sort_matrix(core, each):
    left = lax.broadcasted_iota(jnp.int32, (256, 256), 0)
    right = lax.broadcasted_iota(jnp.int32, (256, 256), 1)
    place = right % 128
    source = (place // each * 2 + (core + 1 + right // 128) % 2) * each + place % each
    return (left == source).astype(jnp.bfloat16)


def sort_cores(value, matrix, out_ref, start):
    half = out_ref.shape[1] // 2
    for n in range(value.shape[1] // 256):
        both = jnp.dot(value[:, 256 * n : 256 * (n + 1)], matrix, preferred_element_type=jnp.float32)
        at = start + 128 * n
        out_ref[:, at : at + 128] = both[:, :128].astype(jnp.bfloat16)
        out_ref[:, half + at : half + at + 128] = both[:, 128:].astype(jnp.bfloat16)


def sort_kernel(each, core_ref, value_ref, out_ref):
    sort_cores(value_ref[...], sort_matrix(core_ref[0], each), out_ref, 0)


def sorted_cores(value, core, each):
    rows, width = value.shape
    tile = min(512, rows)
    spec = pl.BlockSpec((tile, width), lambda i: (i, 0))
    return pl.pallas_call(
        partial(sort_kernel, each),
        grid=(rows // tile,),
        in_specs=[pl.BlockSpec(memory_space=pltpu.SMEM), spec],
        out_specs=spec,
        out_shape=jax.ShapeDtypeStruct((rows, width), value.dtype),
        cost_estimate=pl.CostEstimate(flops=512 * rows * width, bytes_accessed=4 * rows * width, transcendentals=0),
        name="sort_cores",
    )(core, value)


def after_attention_kernel(each, core_ref, a0_ref, a1_ref, w_ref, x_ref, alpha_ref,
                           branch_ref, h_ref, low_ref, hs_ref, as_ref):
    f32 = jnp.float32
    half = a0_ref.shape[1]
    matrix = sort_matrix(core_ref[0], each)
    branch = jnp.dot(a0_ref[...], w_ref[:half, :], preferred_element_type=f32)
    branch = branch + jnp.dot(a1_ref[...], w_ref[half:, :], preferred_element_type=f32)
    branch_ref[...] = branch
    unit = branch * lax.rsqrt(mean_last(branch * branch) + EPS)
    x = x_ref[...].astype(f32)
    z = x + alpha_ref[...] * (unit - x)
    h = z * lax.rsqrt(mean_last(z * z) + EPS)
    low = h.astype(jnp.bfloat16)
    h_ref[...] = h
    low_ref[...] = low
    sort_cores(low, matrix, hs_ref, 0)
    sort_cores(a0_ref[...], matrix, as_ref, 0)
    sort_cores(a1_ref[...], matrix, as_ref, half // 2)


def after_attention(core, each, att, w_out, tokens, alpha):
    rows, width = tokens.shape
    tile = min(512, rows)
    full = pl.BlockSpec((tile, width), lambda i: (i, 0))
    half = pl.BlockSpec((tile, width // 2), lambda i: (i, 0))
    shape = lambda cols, kind: jax.ShapeDtypeStruct((rows, cols), kind)
    return pl.pallas_call(
        partial(after_attention_kernel, each),
        grid=(rows // tile,),
        in_specs=[
            pl.BlockSpec(memory_space=pltpu.SMEM), half, half,
            pl.BlockSpec((width, width), lambda i: (0, 0)), full, pl.BlockSpec((1, width), lambda i: (0, 0)),
        ],
        out_specs=[full] * 5,
        out_shape=[shape(width, jnp.float32)] * 2 + [shape(width, jnp.bfloat16)] * 3,
        compiler_params=pltpu.CompilerParams(vmem_limit_bytes=40 << 20),
        cost_estimate=pl.CostEstimate(flops=2 * rows * width * width, bytes_accessed=20 * rows * width, transcendentals=0),
        name="after_attention",
    )(core, *att, w_out, tokens, alpha)


def sigmoid(value):
    return 0.5 * jnp.tanh(0.5 * value) + 0.5


def up_kernel(h_ref, wu_ref, wg_ref, su_ref, sg_ref, up_ref, gate_ref, hid_ref):
    f32 = jnp.float32
    bf16 = jnp.bfloat16
    up = jnp.dot(h_ref[...], wu_ref[...], preferred_element_type=f32)
    gate = jnp.dot(h_ref[...], wg_ref[...], preferred_element_type=f32)
    value = gate * sg_ref[...]
    up_ref[...] = up.astype(bf16)
    gate_ref[...] = gate.astype(bf16)
    hid_ref[...] = (up * su_ref[...] * (value * sigmoid(value))).astype(bf16)


def feed_up(h_low, w, scale_up, scale_gate):
    rows, width = h_low.shape
    total = scale_up.shape[1]
    block = min(512, total)
    steps = total // block
    shape = jax.ShapeDtypeStruct((rows, total), jnp.bfloat16)
    out = pl.BlockSpec((rows, block), lambda j: (0, j))
    scale = pl.BlockSpec((1, block), lambda j: (0, j))
    return pl.pallas_call(
        up_kernel,
        grid=(steps,),
        in_specs=[
            pl.BlockSpec((rows, width), lambda j: (0, 0)),
            pl.BlockSpec((width, block), lambda j: (0, j)),
            pl.BlockSpec((width, block), lambda j: (0, steps + j)),
            scale, scale,
        ],
        out_specs=[out] * 3,
        out_shape=[shape] * 3,
        compiler_params=pltpu.CompilerParams(vmem_limit_bytes=48 << 20),
        cost_estimate=pl.CostEstimate(flops=4 * rows * width * total, bytes_accessed=2 * (rows * width + 2 * width * total + 3 * rows * total), transcendentals=rows * total),
        name="feed_up",
    )(h_low, w, w, scale_up, scale_gate)


def finish_kernel(scale_ref, hid_ref, wd_ref, m0_ref, h_ref, t_ref, mask_ref, alpha_ref,
                  out_ref, gm_ref, gz_ref, ga_ref, loss_ref):
    f32 = jnp.float32
    m1 = jnp.dot(hid_ref[...], wd_ref[...], preferred_element_type=f32)
    branch = jnp.concatenate([m0_ref[...], m1], axis=1)
    factor = lax.rsqrt(mean_last(branch * branch) + EPS)
    unit = branch * factor
    h1 = h_ref[...]
    alpha = alpha_ref[...]
    z = h1 + alpha * (unit - h1)
    z_factor = lax.rsqrt(mean_last(z * z) + EPS)
    h2 = z * z_factor
    out_ref[...] = h2.astype(jnp.bfloat16)
    diff = h2 - t_ref[...].astype(f32)
    masked = mask_ref[...] * diff
    grad = scale_ref[0] * masked
    gz = z_factor * (grad - h2 * mean_last(grad * h2))
    gz_ref[...] = (1.0 - alpha) * gz
    back = alpha * gz
    gm_ref[...] = (factor * (back - unit * mean_last(back * unit))).astype(jnp.bfloat16)

    @pl.when(pl.program_id(0) == 0)
    def _():
        ga_ref[...] = jnp.zeros_like(ga_ref)
        loss_ref[...] = jnp.zeros_like(loss_ref)

    ga_ref[...] += jnp.sum(gz * (unit - h1), axis=0, keepdims=True)
    loss_ref[...] += jnp.sum(masked * diff, axis=0, keepdims=True)


def finish(scale, hidden, wd, m0, h1, teacher, mask, alpha):
    rows, ff = hidden.shape
    width = h1.shape[1]
    tile = min(512, rows)
    full = pl.BlockSpec((tile, width), lambda i: (i, 0))
    row = pl.BlockSpec((1, width), lambda i: (0, 0))
    line = jax.ShapeDtypeStruct((1, width), jnp.float32)
    return pl.pallas_call(
        finish_kernel,
        grid=(rows // tile,),
        in_specs=[
            pl.BlockSpec(memory_space=pltpu.SMEM),
            pl.BlockSpec((tile, ff), lambda i: (i, 0)),
            pl.BlockSpec((ff, wd.shape[1]), lambda i: (0, 0)),
            pl.BlockSpec((tile, width - wd.shape[1]), lambda i: (i, 0)),
            full, full, pl.BlockSpec((tile, 1), lambda i: (i, 0)), row,
        ],
        out_specs=[full, full, full, row, row],
        out_shape=[
            jax.ShapeDtypeStruct((rows, width), jnp.bfloat16),
            jax.ShapeDtypeStruct((rows, width), jnp.bfloat16),
            jax.ShapeDtypeStruct((rows, width), jnp.float32),
            line, line,
        ],
        compiler_params=pltpu.CompilerParams(vmem_limit_bytes=56 << 20),
        cost_estimate=pl.CostEstimate(flops=2 * rows * ff * wd.shape[1], bytes_accessed=2 * rows * ff + 2 * ff * wd.shape[1] + 16 * rows * width, transcendentals=0),
        name="finish",
    )(scale, hidden, wd, m0, h1, teacher, mask, alpha)


def down_back_kernel(g_ref, w0_ref, w1_ref, up_ref, gate_ref, su_ref, sg_ref, gu_ref, gg_ref, gsu_ref, gsg_ref):
    f32 = jnp.float32
    bf16 = jnp.bfloat16
    half = w0_ref.shape[1]
    su = su_ref[...]
    sg = sg_ref[...]
    back = dot_last(g_ref[:, :half], w0_ref[...]) + dot_last(g_ref[:, half:], w1_ref[...])
    up = up_ref[...].astype(f32)
    gate = gate_ref[...].astype(f32)
    value = gate * sg
    sig = sigmoid(value)
    active = value * sig
    with_active = back * active
    g_value = back * up * su * (sig + active * (1.0 - sig))
    gu_ref[...] = (with_active * su).astype(bf16)
    gg_ref[...] = (g_value * sg).astype(bf16)
    gsu_ref[...] = jnp.sum(with_active * up, axis=0, keepdims=True)
    gsg_ref[...] = jnp.sum(g_value * gate, axis=0, keepdims=True)


def down_back(g, wd, up, gate, scale_up, scale_gate):
    rows, width = g.shape
    ff = up.shape[1]
    block = min(512, ff)
    col = pl.BlockSpec((rows, block), lambda j: (0, j))
    line = pl.BlockSpec((1, block), lambda j: (0, j))
    weight = pl.BlockSpec((block, width // 2), lambda j: (j, 0))
    big = jax.ShapeDtypeStruct((rows, ff), jnp.bfloat16)
    small = jax.ShapeDtypeStruct((1, ff), jnp.float32)
    return pl.pallas_call(
        down_back_kernel,
        grid=(ff // block,),
        in_specs=[pl.BlockSpec((rows, width), lambda j: (0, 0)), weight, weight, col, col, line, line],
        out_specs=[col, col, line, line],
        out_shape=[big, big, small, small],
        compiler_params=pltpu.CompilerParams(vmem_limit_bytes=48 << 20),
        cost_estimate=pl.CostEstimate(flops=2 * rows * ff * width, bytes_accessed=8 * rows * ff + 2 * ff * width, transcendentals=rows * ff),
        name="down_back",
    )(g, *wd, up, gate, scale_up, scale_gate)


def up_back_kernel(steps, gu_ref, gg_ref, wu_ref, wg_ref, gz_ref, branch_ref, x_ref, alpha_ref, gb_ref, gx_ref, ga_ref, acc):
    f32 = jnp.float32
    step = pl.program_id(0)

    @pl.when(step == 0)
    def _():
        acc[...] = gz_ref[...]

    acc[...] += dot_last(gu_ref[...], wu_ref[...]) + dot_last(gg_ref[...], wg_ref[...])

    @pl.when(step == steps - 1)
    def _():
        alpha = alpha_ref[...]
        tile = min(256, acc.shape[0])
        total = jnp.zeros(ga_ref.shape, f32)
        for at in range(0, acc.shape[0], tile):
            branch = branch_ref[at : at + tile, :]
            a_factor = lax.rsqrt(mean_last(branch * branch) + EPS)
            unit = branch * a_factor
            x = x_ref[at : at + tile, :].astype(f32)
            z = x + alpha * (unit - x)
            z_factor = lax.rsqrt(mean_last(z * z) + EPS)
            h = z * z_factor
            grad = acc[at : at + tile, :]
            gz = z_factor * (grad - h * mean_last(grad * h))
            total = total + jnp.sum(gz * (unit - x), axis=0, keepdims=True)
            back = alpha * gz
            gb_ref[at : at + tile, :] = (a_factor * (back - unit * mean_last(back * unit))).astype(jnp.bfloat16)
            gx_ref[at : at + tile, :] = (1.0 - alpha) * gz
        ga_ref[...] = total


def up_back(g_up, g_gate, w, gz, branch, tokens, alpha):
    rows, width = tokens.shape
    ff = g_up.shape[1]
    block = min(1024, ff)
    steps = ff // block
    once = pl.Buffered(1)
    whole = lambda: pl.BlockSpec((rows, width), lambda s: (0, 0), pipeline_mode=once)
    col = pl.BlockSpec((rows, block), lambda s: (0, s))
    line = pl.BlockSpec((1, width), lambda s: (0, 0))
    return pl.pallas_call(
        partial(up_back_kernel, steps),
        grid=(steps,),
        in_specs=[
            col, col, pl.BlockSpec((width, block), lambda s: (0, s)),
            pl.BlockSpec((width, block), lambda s: (0, s + steps)),
            whole(), whole(), whole(), line,
        ],
        out_specs=[whole(), whole(), line],
        out_shape=[
            jax.ShapeDtypeStruct((rows, width), jnp.bfloat16),
            jax.ShapeDtypeStruct((rows, width), jnp.float32),
            jax.ShapeDtypeStruct((1, width), jnp.float32),
        ],
        scratch_shapes=[pltpu.VMEM((rows, width), jnp.float32)],
        compiler_params=pltpu.CompilerParams(vmem_limit_bytes=60 << 20),
        cost_estimate=pl.CostEstimate(flops=4 * rows * width * ff, bytes_accessed=4 * ff * (rows + width) + 14 * rows * width, transcendentals=0),
        name="up_back",
    )(g_up, g_gate, w, w, gz, branch, tokens, alpha)


def down_grad_kernel(each, core_ref, h_ref, g_ref, other_ref, own_ref, whole_ref):
    whole_ref[...] = dot_first(h_ref[...], g_ref[...])
    core = core_ref[0]
    for n in range(h_ref.shape[1] // (2 * each)):
        for out_ref, which in ((other_ref, 1 - core), (own_ref, core)):
            start = pl.multiple_of((2 * n + which) * each, each)
            out_ref[n * each : (n + 1) * each, :] = whole_ref[pl.ds(start, each), :].astype(jnp.bfloat16)


def down_grad(core, hidden, g, groups):
    rows, ff = hidden.shape
    width = g.shape[1]
    each = ff // (2 * groups)
    block = min(1024, ff)
    out = pl.BlockSpec((block // 2, width), lambda i: (i, 0))
    shape = jax.ShapeDtypeStruct((ff // 2, width), jnp.bfloat16)
    return pl.pallas_call(
        partial(down_grad_kernel, each),
        grid=(ff // block,),
        in_specs=[
            pl.BlockSpec(memory_space=pltpu.SMEM),
            pl.BlockSpec((rows, block), lambda i: (0, i)),
            pl.BlockSpec((rows, width), lambda i: (0, 0)),
        ],
        out_specs=[out, out],
        out_shape=[shape, shape],
        scratch_shapes=[pltpu.VMEM((block, width), jnp.float32)],
        compiler_params=pltpu.CompilerParams(vmem_limit_bytes=40 << 20),
        cost_estimate=pl.CostEstimate(flops=2 * rows * ff * width, bytes_accessed=2 * rows * ff + 2 * ff * width + 2 * rows * width, transcendentals=0),
        name="down_grad",
    )(core, hidden, g)


def row_grad_kernel(left_ref, *refs):
    rights, (other_ref, own_ref) = refs[:-2], refs[-2:]
    half = other_ref.shape[0]
    at = 0
    for right in rights:
        cols = right.shape[1]
        both = dot_first(left_ref[...], right[...])
        other_ref[:, at : at + cols] = both[:half, :].astype(jnp.bfloat16)
        own_ref[:, at : at + cols] = both[half:, :].astype(jnp.bfloat16)
        at += cols


def row_grad(left, right):
    rows, width = left.shape
    cols = right.shape[1]
    block = min(512, cols)
    out = pl.BlockSpec((width // 2, block), lambda j: (0, j))
    shape = jax.ShapeDtypeStruct((width // 2, cols), jnp.bfloat16)
    return pl.pallas_call(
        row_grad_kernel,
        grid=(cols // block,),
        in_specs=[
            pl.BlockSpec((rows, width), lambda j: (0, 0)),
            pl.BlockSpec((rows, block), lambda j: (0, j)),
        ],
        out_specs=[out, out],
        out_shape=[shape, shape],
        compiler_params=pltpu.CompilerParams(vmem_limit_bytes=40 << 20),
        cost_estimate=pl.CostEstimate(flops=2 * rows * width * cols, bytes_accessed=2 * (rows * width + width * cols + rows * cols), transcendentals=0),
        name="row_grad",
    )(left, right)


def heads_grad(left, parts):
    rows, width = left.shape
    cols = parts[0].shape[2]
    count = len(parts)
    out = pl.BlockSpec((width // 2, cols * count), lambda j: (0, j))
    shape = jax.ShapeDtypeStruct((width // 2, 3 * cols * count), jnp.bfloat16)
    return pl.pallas_call(
        row_grad_kernel,
        grid=(3,),
        in_specs=[pl.BlockSpec((rows, width), lambda j: (0, 0))]
        + [pl.BlockSpec((pl.Squeezed(), rows, cols), lambda j: (j, 0, 0))] * count,
        out_specs=[out, out],
        out_shape=[shape, shape],
        compiler_params=pltpu.CompilerParams(vmem_limit_bytes=40 << 20),
        cost_estimate=pl.CostEstimate(flops=6 * rows * width * cols * count, bytes_accessed=2 * (rows * width + 3 * (width + rows) * cols * count), transcendentals=0),
        name="heads_grad",
    )(left, *parts)


def input_grad_kernel(base_ref, *refs):
    out_ref = refs[-1]
    count = len(refs) // 3
    total = base_ref[...]
    for n in range(count):
        first, second, w = refs[n * 3 : n * 3 + 3]
        cols = first.shape[2]
        for p in range(3):
            at = 2 * p * cols
            total = total + dot_last(first[p], w[:, at : at + cols])
            total = total + dot_last(second[p], w[:, at + cols : at + 2 * cols])
    out_ref[...] = total


def input_grad(base, parts, weights):
    rows, width = base.shape
    tile = min(256, width)
    out = pl.BlockSpec((rows, tile), lambda j: (0, j))
    specs, operands = [], []
    for n, w in enumerate(weights):
        for part in parts[2 * n : 2 * n + 2]:
            specs.append(pl.BlockSpec(part.shape, lambda j: (0, 0, 0), pipeline_mode=pl.Buffered(1)))
            operands.append(part)
        specs.append(pl.BlockSpec((tile, w.shape[1]), lambda j: (j, 0)))
        operands.append(w)
    flops = 2 * rows * width * sum(w.shape[1] for w in weights)
    return pl.pallas_call(
        input_grad_kernel,
        grid=(width // tile,),
        in_specs=[out] + specs,
        out_specs=out,
        out_shape=jax.ShapeDtypeStruct((rows, width), jnp.float32),
        compiler_params=pltpu.CompilerParams(vmem_limit_bytes=48 << 20),
        cost_estimate=pl.CostEstimate(flops=flops, bytes_accessed=20 * rows * width, transcendentals=0),
        name="input_grad",
    )(base, *operands)


def slots_kernel(count, uses, slots_ref, keep_ref, got_ref, *refs):
    extras, out_ref, acc = refs[:-2], refs[-2], refs[-1]
    f32 = jnp.float32
    acc[...] = keep_ref[...].astype(f32) + got_ref[...].astype(f32)
    for n, extra in enumerate(extras):
        takers = [i for i in range(count) if uses[n][i] is not None]
        if len(takers) == count:
            acc[...] += extra[...].astype(f32)
            continue
        for i in takers:

            @pl.when(pl.program_id(0) == i)
            def _(extra=extra):
                acc[...] += extra[...].astype(f32)

    out_ref[...] = acc[...].astype(out_ref.dtype)


def add_slots(keep, got, rows, slots, extras=()):
    count = len(slots)
    cols = keep.shape[1]
    uses = [use for _, use in extras]
    specs = [pl.BlockSpec((rows, cols), lambda i, s: (s[i], 0))] * 2
    for _, use in extras:
        first = next(u for u in use if u is not None)
        if all(u is None or u == first for u in use):
            specs.append(pl.BlockSpec((rows, cols), lambda i, s, first=first: (first, 0)))
        else:
            assert use == list(range(count))
            specs.append(pl.BlockSpec((rows, cols), lambda i, s: (i, 0)))
    grid = pltpu.PrefetchScalarGridSpec(
        num_scalar_prefetch=1,
        grid=(count,),
        in_specs=specs,
        out_specs=pl.BlockSpec((rows, cols), lambda i, s: (i, 0)),
        scratch_shapes=[pltpu.VMEM((rows, cols), jnp.float32)],
    )
    return pl.pallas_call(
        partial(slots_kernel, count, uses),
        grid_spec=grid,
        out_shape=jax.ShapeDtypeStruct((count * rows, cols), keep.dtype),
        compiler_params=pltpu.CompilerParams(vmem_limit_bytes=40 << 20),
        cost_estimate=pl.CostEstimate(flops=0, bytes_accessed=8 * count * rows * cols, transcendentals=0),
        name="add_slots",
    )(jnp.stack(slots).astype(jnp.int32), keep, got, *[e for e, _ in extras])


def body(
    tokens,
    teacher,
    valid,
    segments,
    positions,
    w_qkv,
    w_out,
    w_upgate,
    w_down,
    s_qk,
    alpha_attn,
    s_up,
    s_gate,
    alpha_mlp,
):
    f32 = jnp.float32
    bf16 = jnp.bfloat16
    at = Place()
    rows, width = tokens.shape
    ff = w_upgate.shape[1] // 2
    each = w_out.shape[0]
    groups = at.shards // NC
    core = at.core.reshape(1).astype(jnp.int32)
    half = width // 2
    pairs = half // PAIR
    segs = segments.reshape(rows, 1)

    def columns(w, starts, size):
        return jnp.concatenate([w[:, s : s + size] for s in starts], axis=1)

    chunks = [columns(w_qkv, [p * width + n * half for p in range(3)], half) for n in range(2)]
    chunks.append(w_out)
    full_up = lax.all_gather(w_upgate, "shard", axis=0, tiled=True)
    chunks += [w_down[:, :half], w_down[:, half:]]

    gather = Gather(at, chunks)
    gate = []
    for tick in range(4):
        gate = gather.tick(tick, gate)
    vectors = gather_vectors(at, (s_qk, alpha_attn, s_up, s_gate, alpha_mlp))
    f_sqk, f_aa, f_su, f_sg, f_am = (v.astype(f32).reshape(1, -1) for v in vectors)
    mask = valid.astype(f32)
    count = jnp.maximum(sum_everywhere(at, jnp.full((8, 128), jnp.sum(mask)))[0, 0], 1.0)
    scale = (2.0 * rows * at.reps * at.shards / count).reshape(1)
    cosine, sine = rotary_wide(positions.reshape(rows))
    x_sorted = sorted_cores(tokens, core, each)
    gate += [x_sorted, cosine, f_sqk, scale]

    def dot(left, right):
        return jnp.dot(left, right, preferred_element_type=f32).astype(bf16)

    weights, qkv, att, lse = {}, [], [], []
    for n in range(2):
        moved = gather.tick(4 + n, gate)
        weights[n] = gather.full(n)
        qkv.append(dot(after(tokens, gate), weights[n]))
        out, sums = attention(qkv[n], cosine, sine, f_sqk, segs, n * half)
        att.append(out)
        lse.append(sums)
        gate = moved + [out]
    moved = gather.tick(6, gate)
    weights[2] = gather.full(2)
    att = [after(a, gate) for a in att]
    branch_a, h_one, h_low, h_sorted, att_sorted = after_attention(core, each, att, weights[2], tokens, f_aa)
    gate = moved + [h_low]
    moved = gather.tick(7, gate)
    up, gate_part, hidden = feed_up(after(h_low, moved), full_up, f_su, f_sg)
    down = [gather.full(3), gather.full(4)]
    m_first = jnp.dot(hidden, down[0], preferred_element_type=f32)
    output, g_bm, gz, grad_am, loss_rows = finish(
        scale, hidden, down[1], m_first, h_one, teacher, mask.reshape(rows, 1), f_am
    )

    lanes = []
    waiting = {}

    def window(gate, enter):
        moved = []
        for name in enter:
            lanes.append(waiting[name])
        for chunk in lanes:
            if chunk.stage < 5:
                moved += chunk.step(gate)
        return moved

    def start(name, left, right, gate):
        waiting[name] = Reduce(at, *row_grad(left, after(right, gate)))
        return [waiting[name].send, waiting[name].keep]

    def dot_rows(left, right):
        return lax.dot_general(left, right, (((0,), (0,)), ((), ())), preferred_element_type=f32).astype(bf16)

    sides = down_grad(core, hidden, g_bm, groups)
    waiting["down"] = Reduce(at, *sides)
    gate = list(sides)
    moved = window(gate, ["down"])
    g_up, g_gate, grad_su, grad_sg = down_back(after(g_bm, gate), down, up, gate_part, f_su, f_sg)
    gate = moved + [g_up]
    moved = window(gate, [])
    own_up = lax.psum_scatter(dot_rows(after(h_low, gate), g_up), "shard", scatter_dimension=0, tiled=True)
    done = start("gate", h_sorted, g_gate, gate)
    gate = moved + done
    moved = window(gate, ["gate"])
    g_ba, gx_base, grad_aa = up_back(after(g_up, gate), g_gate, full_up, gz, branch_a, tokens, f_aa)
    gate = moved + [g_ba]

    g3, g_scale = {}, []

    def back(n, gate):
        part = pairs // 2
        out, sums = attention_back(
            qkv[n // 2], att[n // 2], after(g_att, gate), lse[n // 2], cosine, sine, f_sqk, segs,
            n // 2 * half, n % 2 * part, part,
        )
        g3[n] = out
        g_scale.append(sums[:, 0, :].reshape(-1))
        return [out]

    def start_qkv(n, gate):
        sides = heads_grad(after(x_sorted, gate), [g3[2 * n], g3[2 * n + 1]])
        waiting[f"qkv{n}"] = Reduce(at, *sides)
        return list(sides)

    moved = window(gate, [])
    g_att = lax.dot_general(
        after(g_ba, gate), weights[2], (((1,), (1,)), ((), ())), preferred_element_type=f32
    ).astype(bf16)
    done = start("out", att_sorted, g_ba, gate)
    gate = moved + done + back(0, gate)
    moved = window(gate, ["out"])
    gate = moved + back(1, gate)
    moved = window(gate, [])
    done = start_qkv(0, gate)
    gate = moved + done + back(2, gate)
    moved = window(gate, ["qkv0"])
    gate = moved + back(3, gate)
    moved = window(gate, [])
    gate = moved + start_qkv(1, gate)
    moved = window(gate, ["qkv1"])
    grad_x = input_grad(after(gx_base, gate), [g3[n] for n in range(4)], [weights[0], weights[1]])
    parts = [
        jnp.concatenate(g_scale), grad_aa.reshape(-1), grad_su.reshape(-1), grad_sg.reshape(-1),
        grad_am.reshape(-1), jnp.sum(loss_rows).reshape(1),
    ]
    sizes = [p.shape[0] for p in parts]
    flat = jnp.concatenate(parts)
    tall = -(-flat.shape[0] // 1024) * 8
    flat = jnp.pad(flat, (0, tall * 128 - flat.shape[0])).reshape(tall, 128)
    flat = sum_everywhere(at, flat).reshape(-1)
    gate = moved + [grad_x]
    while any(chunk.stage < 5 for chunk in lanes):
        gate = window(gate, [])
    owned = []
    place = 0
    for size in sizes[:-1]:
        mine = size // at.shards
        owned.append(lax.dynamic_slice_in_dim(flat, place + at.shard * mine, mine))
        place += size
    loss = flat[place] / count
    total = {name: chunk.total() for name, chunk in waiting.items()}
    own_up = after(own_up, gate)
    own_up = over_copies(at, own_up.astype(f32), 1)
    halves = lambda value: [value[:, p * half : (p + 1) * half] for p in range(3)]
    q0, q1 = halves(total["qkv0"]), halves(total["qkv1"])
    own_qkv = jnp.concatenate([part for pair in zip(q0, q1) for part in pair], axis=1)
    own_up = jnp.concatenate([own_up, total["gate"]], axis=1)
    return (output, loss, grad_x, own_qkv, total["out"], own_up, total["down"], *owned)


def solution(mesh):
    return jax.shard_map(
        body,
        mesh=mesh,
        in_specs=(
            P(("rep", "shard"), None),
            P(("rep", "shard"), None),
            P(("rep", "shard")),
            P(("rep", "shard"), None),
            P(("rep", "shard"), None),
            P("shard", None),
            P("shard", None),
            P("shard", None),
            P("shard", None),
            P("shard"),
            P("shard"),
            P("shard"),
            P("shard"),
            P("shard"),
        ),
        out_specs=(
            P(("rep", "shard"), None),
            P(),
            P(("rep", "shard"), None),
            P("shard", None),
            P("shard", None),
            P("shard", None),
            P("shard", None),
            P("shard"),
            P("shard"),
            P("shard"),
            P("shard"),
            P("shard"),
        ),
        check_vma=False,
    )
```

```python
from functools import partial
import math

import jax
import jax.numpy as jnp
from jax import lax
from jax.experimental import pallas as pl
from jax.experimental.pallas import tpu as pltpu
from jax.sharding import PartitionSpec as P

EPS = 1e-06
AXES = ("rep", "shard")
NZ = 4
NC = 2


class Place:
    def __init__(self):
        self.reps = lax.axis_size("rep")
        self.shards = lax.axis_size("shard")
        self.nx = self.shards // (NZ * NC)
        self.pairs = self.reps % 2 == 0
        rep = lax.axis_index("rep")
        shard = lax.axis_index("shard")
        self.rep = rep
        self.shard = shard
        self.y = rep % 2
        self.core = shard % NC
        self.x = (shard // NC) % self.nx
        self.z = shard // (NC * self.nx)

    def moves(self, step):
        pairs = []
        for rep in range(self.reps):
            for z in range(NZ):
                for x in range(self.nx):
                    for core in range(NC):
                        to_rep, to_z, to_x, to_core = step(rep, z, x, core)
                        pairs.append(
                            (
                                rep * self.shards + (z * self.nx + x) * NC + core,
                                to_rep * self.shards + (to_z * self.nx + to_x) * NC + to_core,
                            )
                        )
        return pairs

    def near_z(self, value):
        return lax.ppermute(value, AXES, self.moves(lambda r, z, x, c: (r, z ^ 1, x, c)))

    def far_z(self, value):
        return lax.ppermute(value, AXES, self.moves(lambda r, z, x, c: (r, z ^ (2 + r % 2), x, c)))

    def along_x(self, value, j):
        return lax.ppermute(value, AXES, self.moves(lambda r, z, x, c: (r, z, x ^ j, c)))

    def along_y(self, value):
        return lax.ppermute(value, AXES, self.moves(lambda r, z, x, c: (r ^ 1, z, x, c)))

    def other_core(self, value):
        return lax.ppermute(value, AXES, self.moves(lambda r, z, x, c: (r, z, x, c ^ 1)))

    def flat(self, value, bit):
        count = self.reps * self.shards
        return lax.ppermute(value, AXES, [(i, i ^ bit) for i in range(count)])

    def slot(self, k, j):
        return (self.z ^ k) * self.nx + (self.x ^ j)


def tie(*values):
    return lax.optimization_barrier(values)


def place_kernel(count, slots, *refs):
    pieces, out = refs[:-1], refs[-1]
    for i in range(count):
        rows = pieces[i].shape[0]
        at = pl.multiple_of(slots[i] * rows, rows)
        out[pl.ds(at, rows), :] = pieces[i][...]


def assemble(pieces, slots, rows_out):
    cols = pieces[0].shape[1]
    size = rows_out * cols * pieces[0].dtype.itemsize
    return pl.pallas_call(
        partial(place_kernel, len(pieces)),
        out_shape=jax.ShapeDtypeStruct((rows_out, cols), pieces[0].dtype),
        in_specs=[pl.BlockSpec(memory_space=pltpu.SMEM)]
        + [pl.BlockSpec(memory_space=pltpu.VMEM)] * len(pieces),
        out_specs=pl.BlockSpec(memory_space=pltpu.VMEM),
        compiler_params=pltpu.CompilerParams(vmem_limit_bytes=2 * size + (4 << 20)),
        cost_estimate=pl.CostEstimate(flops=0, bytes_accessed=2 * size, transcendentals=0),
    )(slots, *pieces)


def weave_kernel(columns, core, half, other, *refs):
    out, sems = refs[-2], refs[-1]
    at = core[0]
    copies = []
    for n, (source, target, size) in enumerate(columns):
        cols = pl.ds(target, size)
        copies.append(pltpu.make_async_copy(half.at[:, :, source : source + size], out.at[:, at, :, cols], sems.at[0, n]))
        copies.append(pltpu.make_async_copy(other.at[:, :, source : source + size], out.at[:, 1 - at, :, cols], sems.at[1, n]))
    for copy in copies:
        copy.start()
    for copy in copies:
        copy.wait()


def weave(half, other, core, groups, columns, total, before):
    rows, cols = half.shape
    each = rows // groups
    size = rows * cols * half.dtype.itemsize
    shape = (groups, each, cols)
    full = (groups, 2, each, total)
    return pl.pallas_call(
        partial(weave_kernel, columns),
        out_shape=jax.ShapeDtypeStruct(full, half.dtype),
        in_specs=[
            pl.BlockSpec(memory_space=pltpu.SMEM),
            pl.BlockSpec(memory_space=pltpu.VMEM),
            pl.BlockSpec(memory_space=pltpu.VMEM),
        ]
        + [pl.BlockSpec(memory_space=pl.ANY)] * len(before),
        out_specs=pl.BlockSpec(memory_space=pl.ANY),
        scratch_shapes=[pltpu.SemaphoreType.DMA((2, len(columns)))],
        input_output_aliases={3: 0} if before else {},
        compiler_params=pltpu.CompilerParams(vmem_limit_bytes=2 * size + (4 << 20)),
        cost_estimate=pl.CostEstimate(flops=0, bytes_accessed=4 * size, transcendentals=0),
        name="weave",
    )(core, half.reshape(shape), other.reshape(shape), *[b.reshape(full) for b in before]).reshape(2 * rows, total)


class Gather:
    def __init__(self, at, chunks):
        self.at = at
        self.ready = list(chunks)
        self.near, self.far, self.over_x, self.over_y = {}, {}, {}, {}
        self.own, self.other = {}, {}
        self.groups = NZ * at.nx
        self.core = at.core.reshape(1).astype(jnp.int32)

    def tick(self, tick, gate):
        at = self.at
        count = len(self.ready)
        offsets = range(1, at.nx)
        y = at.y
        ended = []
        self.sends = []
        if tick < count:
            piece = after(self.ready[tick], gate)
            self.ready[tick] = piece
            self.near[tick] = at.near_z(piece)
            self.far[tick] = at.far_z(piece)
            ended += [self.near[tick], self.far[tick]]
        i = tick - 1
        if 0 <= i < count:
            piece = self.ready[i]
            rows = piece.shape[0]
            halves = [
                lax.dynamic_slice_in_dim(part, y * (rows // 2), rows // 2, axis=0) for part in (piece, self.near[i])
            ]
            send = after(jnp.concatenate(halves + [self.far[i]], axis=0), gate)
            self.sends.append(send)
            self.over_x[i] = [at.along_x(send, j) for j in offsets]
            ended += self.over_x[i]
        i = tick - 2
        if 0 <= i < count:
            rows = self.ready[i].shape[0]
            sends = [self.far[i]]
            sends += self.over_x[i]
            send = after(jnp.concatenate(sends, axis=0), gate)
            self.sends.append(send)
            self.over_y[i] = at.along_y(send)
            ended += [self.over_y[i]]
        i = tick - 3
        if 0 <= i < count:
            rows = self.ready[i].shape[0]
            half = rows // 2
            got = self.over_y[i]
            pieces = [self.ready[i], self.near[i], self.far[i], got[:rows]]
            slots = [at.slot(0, 0), at.slot(1, 0), at.slot(2 + y, 0), at.slot(3 - y, 0)]
            place = rows
            for mine, j in zip(self.over_x[i], offsets):
                for got_here, side in ((mine, y), (got[place : place + 2 * rows], 1 - y)):
                    pieces += [got_here[:half], got_here[half:rows], got_here[rows:]]
                    slots += [at.slot(0, j) * 2 + side, at.slot(1, j) * 2 + side, at.slot(2 + side, j)]
                place += 2 * rows
            self.own[i] = assemble(pieces, jnp.stack(slots).astype(jnp.int32), self.groups * rows)
            self.sends.append(self.own[i])
            self.other[i] = at.other_core(after(self.own[i], gate))
            ended += [self.other[i]]
        return ended

    def full(self, i, columns=None, total=None, before=()):
        cols = self.own[i].shape[1]
        columns = columns or [(0, 0, cols)]
        return weave(self.own[i], self.other[i], self.core, self.groups, columns, total or cols, before)


def after(value, gate):
    return tie(value, *gate)[0] if gate else value


class Reduce:
    def __init__(self, at, send, keep):
        self.at = at
        self.send = send
        self.keep = keep
        self.rows = keep.shape[0] // (NZ * at.nx)
        self.stage = 0

    def add(self, gate, places, plan, terms=()):
        slots = [self.at.slot(k, j) for k, j in places]
        self.sends = list(add_slots(after(self.keep, gate), self.got, self.rows, slots, plan, terms))
        return self.sends

    def step(self, gate):
        at = self.at
        offsets = range(1, at.nx)
        y = at.y
        stage = self.stage
        self.stage += 1
        if stage == 0:
            self.sends = []
            self.got = at.other_core(after(self.send, gate))
            return [self.got]
        if stage == 1:
            (send,) = self.add(gate, [(3 - y, j) for j in range(at.nx)], [[[]] * at.nx])
            self.got_y = at.along_y(send)
            return [self.got_y]
        if stage == 2:
            places, plan = [], []
            for j in offsets:
                places += [(0, j), (1, j), (2 + y, j)]
                plan.append([[], [], [(0, j)]])
            sends = self.add(gate, places, plan, [self.got_y])
            self.got_x = [at.along_x(send, j) for send, j in zip(sends, offsets)]
            return self.got_x
        if stage == 3:
            count = len(self.got_x)
            near, far = self.add(
                gate,
                [(1, 0), (2 + y, 0)],
                [[[(1 + n, 1) for n in range(count)]], [[(0, 0)] + [(1 + n, 2) for n in range(count)]]],
                [self.got_y] + self.got_x,
            )
            self.near = at.near_z(near)
            self.far = at.far_z(far)
            return [self.near, self.far]
        if stage == 4:
            terms = [self.near, self.far] + self.got_x
            (self.mine,) = self.add(gate, [(0, 0)], [[[(n, 0) for n in range(len(terms))]]], terms)
            self.last = at.along_y(self.mine)
            return [self.last]
        return []

    def total(self):
        return over_copies(self.at, self.mine.astype(jnp.float32) + self.last.astype(jnp.float32), 2)


def over_copies(at, total, bit):
    while bit < at.reps:
        total = total + at.flat(total.astype(jnp.bfloat16), bit * at.shards).astype(jnp.float32)
        bit *= 2
    return total


class Sum:
    def __init__(self, at, value):
        self.at = at
        self.value = value
        self.bit = 1

    def step(self, gate):
        if self.bit >= self.at.reps * self.at.shards:
            return []
        value = after(self.value, gate)
        self.value = value + self.at.flat(value, self.bit)
        self.bit *= 2
        return [self.value]

    def total(self):
        while self.step([]):
            pass
        return self.value


LOG2E = 1.4426950408889634
HEAD = 64
PAIR = 128
ROWS_Q = 256
ROWS_K = 256


def lanes_of(shape):
    return lax.broadcasted_iota(jnp.int32, shape, len(shape) - 1)


def half_turn(value):
    low = lanes_of(value.shape) % HEAD < HEAD // 2
    return jnp.where(low, pltpu.roll(value, PAIR - HEAD // 2, 1), pltpu.roll(value, HEAD // 2, 1))


def swap_matrix():
    left = lax.broadcasted_iota(jnp.int32, (PAIR, PAIR), 0)
    right = lax.broadcasted_iota(jnp.int32, (PAIR, PAIR), 1)
    return (left == (right ^ (HEAD // 2))).astype(jnp.bfloat16)


def two_parts(value):
    high = value.astype(jnp.bfloat16)
    return high, (value - high.astype(jnp.float32)).astype(jnp.bfloat16)


def head_sum(value):
    left = lax.broadcasted_iota(jnp.int32, (2 * PAIR, PAIR), 0) // HEAD % 2
    right = lax.broadcasted_iota(jnp.int32, (2 * PAIR, PAIR), 1) // HEAD
    same = (left == right).astype(jnp.bfloat16)
    parts = jnp.concatenate(two_parts(value), axis=1)
    return jnp.dot(parts, same, preferred_element_type=jnp.float32)


def turned(raw, cosine, sine):
    swapped = jnp.dot(raw, swap_matrix(), preferred_element_type=jnp.float32)
    rot = raw.astype(jnp.float32) * cosine + swapped * sine
    factor = lax.rsqrt(head_sum(rot * rot) + EPS)
    return rot * factor, factor


def only(value, head):
    mine = lanes_of(value.shape) // HEAD == head
    return jnp.where(mine, value, jnp.zeros_like(value))


def dot_last(a, b):
    return lax.dot_general(a, b, (((1,), (1,)), ((), ())), preferred_element_type=jnp.float32)


def dot_first(a, b):
    return lax.dot_general(a, b, (((0,), (0,)), ((), ())), preferred_element_type=jnp.float32)


FAR = -16384.0


def spare_lane(shape, head):
    return lanes_of(shape) - (1 - head) * HEAD


def query_lanes(value, head, segs):
    spare = spare_lane(value.shape, head)
    own = lanes_of(value.shape) // HEAD == head
    marks = (spare >= 0) & (spare < 8) & (spare != segs)
    return jnp.where(own, value.astype(jnp.float32), jnp.where(marks, FAR, 0.0)).astype(value.dtype)


def key_lanes(value, head, segs):
    spare = spare_lane(value.shape, head)
    own = lanes_of(value.shape) // HEAD == head
    return jnp.where(own, value.astype(jnp.float32), (spare == segs).astype(jnp.float32)).astype(value.dtype)


def attend_kernel(temper, q_ref, k_ref, v_ref, cos_ref, sin_ref, scale_ref, seg_ref, out_ref, lse_ref,
                  q_sc, k_sc, v_sc, sum_sc):
    length = q_ref.shape[0]
    bf16 = jnp.bfloat16
    f32 = jnp.float32
    scale = scale_ref[...]
    cosine = cos_ref[...]
    sine = sin_ref[...]
    segs = seg_ref[...]
    q2 = (turned(q_ref[...], cosine, sine)[0] * scale).astype(bf16)
    k2 = (turned(k_ref[...], cosine, sine)[0] * scale).astype(bf16)
    v = v_ref[...]
    ones = jnp.ones_like(v)
    for head in range(2):
        q_sc[head] = query_lanes(q2, head, segs)
        k_sc[head] = key_lanes(k2, head, segs)
        v_sc[head, :, :PAIR] = only(v, head)
        v_sc[head, :, PAIR:] = only(ones, head)
    factor = temper * LOG2E
    size = min(ROWS_Q, length)
    blocks = length // size
    causal = lax.broadcasted_iota(jnp.int32, (size, size), 0) >= lax.broadcasted_iota(
        jnp.int32, (size, size), 1
    )
    for block in range(blocks):
        at = block * size
        for head in range(2):
            keys = k_sc[head, at : at + size, :]
            raw = dot_last(q_sc[head, at:, :], keys)
            expo = causal_top(jnp.exp2(raw * factor), causal).astype(bf16)
            part = jnp.dot(expo, v_sc[head, at : at + size, :], preferred_element_type=f32)
            if block == 0 and head == 0:
                sum_sc[...] = part
            else:
                sum_sc[at:, :] += part
    mass = sum_sc[:, PAIR:]
    out_ref[...] = (sum_sc[:, :PAIR] / mass).astype(bf16)
    lse_ref[...] = jnp.log2(mass)


def causal_top(value, causal):
    size = causal.shape[0]
    edge = jnp.where(causal, value[:size, :], 0.0)
    if value.shape[0] == size:
        return edge
    return jnp.concatenate([edge, value[size:, :]], axis=0)


def causal_bottom(value, causal):
    size = causal.shape[0]
    edge = jnp.where(causal, value[-size:, :], 0.0)
    if value.shape[0] == size:
        return edge
    return jnp.concatenate([value[:-size, :], edge], axis=0)


def pair_spec(length, offset):
    return pl.BlockSpec((length, PAIR), lambda p: (0, p + offset))


def attention(qkv, cosine, sine, scale, segs, offset):
    length, width = qkv.shape[0], qkv.shape[1] // 3
    pairs = width // PAIR
    whole = pl.BlockSpec((length, PAIR), lambda p: (0, 0))
    column = pl.BlockSpec((length, 1), lambda p: (0, 0))
    return pl.pallas_call(
        partial(attend_kernel, math.sqrt(HEAD)),
        grid=(pairs,),
        in_specs=[
            pair_spec(length, 0), pair_spec(length, pairs), pair_spec(length, 2 * pairs),
            whole, whole, pl.BlockSpec((1, PAIR), lambda p: (0, p + offset // PAIR)), column,
        ],
        out_specs=[pair_spec(length, 0), pair_spec(length, 0)],
        scratch_shapes=[
            pltpu.VMEM((2, length, PAIR), jnp.bfloat16),
            pltpu.VMEM((2, length, PAIR), jnp.bfloat16),
            pltpu.VMEM((2, length, 2 * PAIR), jnp.bfloat16),
            pltpu.VMEM((length, 2 * PAIR), jnp.float32),
        ],
        out_shape=[
            far_array((length, width), jnp.bfloat16),
            far_array((length, width), jnp.float32),
        ],
        compiler_params=pltpu.CompilerParams(vmem_limit_bytes=40 << 20),
        cost_estimate=pl.CostEstimate(
            flops=16 * length * length * width // 2, bytes_accessed=8 * length * width,
            transcendentals=length * length * width // HEAD // 2,
        ),
        name="attend",
    )(qkv, qkv, qkv, cosine, sine, scale, segs)


def three_parts(value):
    high = value.astype(jnp.bfloat16).astype(jnp.float32)
    rest = value - high
    mid = rest.astype(jnp.bfloat16).astype(jnp.float32)
    return high, mid, rest - mid


def attend_back_kernel(temper, q_ref, k_ref, v_ref, o_ref, g_ref, cos_ref, sin_ref, scale_ref, seg_ref, lse_ref,
                       g3_ref, gs_ref, q_sc, k_sc, v_sc, g_sc, dq_sc, dk_sc, dv_sc):
    length = q_ref.shape[0]
    bf16 = jnp.bfloat16
    f32 = jnp.float32
    scale = scale_ref[...]
    cosine = cos_ref[...]
    sine = sin_ref[...]
    segs = seg_ref[...]
    qn, q_factor = turned(q_ref[...], cosine, sine)
    kn, k_factor = turned(k_ref[...], cosine, sine)
    q2 = (qn * scale).astype(bf16)
    k2 = (kn * scale).astype(bf16)
    v = v_ref[...]
    grad = g_ref[...]
    spread = head_sum(grad.astype(f32) * o_ref[...].astype(f32))
    factor = temper * LOG2E
    lanes = lanes_of((length, PAIR))
    for head in range(2):
        spare = spare_lane((length, PAIR), head)
        own = lanes // HEAD == head
        parts = three_parts(lse_ref[:, head * HEAD : head * HEAD + 1] * (-1.0 / factor))
        marks = jnp.where((spare >= 0) & (spare < 8) & (spare != segs), FAR, 0.0)
        for n in range(3):
            marks = jnp.where(spare == 8 + n, parts[n], marks)
        q_sc[head] = jnp.where(own, q2.astype(f32), marks).astype(bf16)
        k_sc[head] = jnp.where(
            own, k2.astype(f32), ((spare == segs) | ((spare >= 8) & (spare < 11))).astype(f32)
        ).astype(bf16)
        parts = three_parts(-spread[:, head * HEAD : head * HEAD + 1])
        marks = jnp.zeros((length, PAIR), f32)
        for n in range(3):
            marks = jnp.where(spare == n, parts[n], marks)
        g_sc[head] = jnp.where(own, grad.astype(f32), marks).astype(bf16)
        v_sc[head] = jnp.where(own, v.astype(f32), ((spare >= 0) & (spare < 3)).astype(f32)).astype(bf16)
    size = min(ROWS_K, length)
    causal = lax.broadcasted_iota(jnp.int32, (size, size), 0) <= lax.broadcasted_iota(
        jnp.int32, (size, size), 1
    )
    blocks = length // size
    lanes = lanes_of((size, PAIR)) // HEAD
    for block in range(blocks - 1, -1, -1):
        at = block * size
        end = at + size
        dqs = []
        for head in range(2):
            queries = q_sc[head, at:end, :]
            grads = g_sc[head, at:end, :]
            keys = k_sc[head, :end, :]
            probs = causal_bottom(jnp.exp2(dot_last(keys, queries) * factor), causal)
            ds = (probs * dot_last(v_sc[head, :end, :], grads)).astype(bf16)
            dv = jnp.dot(probs.astype(bf16), grads, preferred_element_type=f32)
            dk = jnp.dot(ds, queries, preferred_element_type=f32)
            dqs.append(dot_first(ds, keys))
            if block == blocks - 1:
                dv_sc[head] = dv
                dk_sc[head] = dk
            else:
                dv_sc[head, :end, :] += dv
                dk_sc[head, :end, :] += dk
        dq_sc[at:end, :] = jnp.where(lanes == 0, dqs[0], dqs[1])
    lanes = lanes_of((length, PAIR)) // HEAD
    g3_ref[2] = jnp.where(lanes == 0, dv_sc[0], dv_sc[1]).astype(bf16)
    dq = dq_sc[...] * temper
    dk = jnp.where(lanes == 0, dk_sc[0], dk_sc[1]) * temper
    gs_ref[0] = jnp.broadcast_to(jnp.sum(dq * qn + dk * kn, axis=0, keepdims=True), (8, PAIR))

    def unturn(grad, unit, unit_factor):
        grad = grad * scale
        rot = unit_factor * (grad - unit * head_sum(grad * unit))
        return (rot * cosine + half_turn(rot * sine)).astype(bf16)

    g3_ref[0] = unturn(dq, qn, q_factor)
    g3_ref[1] = unturn(dk, kn, k_factor)


def attention_back(qkv, out, grad, lse, cosine, sine, scale, segs, offset, first, pairs):
    length, width = qkv.shape[0], qkv.shape[1] // 3
    every = width // PAIR
    base = offset // PAIR
    whole = pl.BlockSpec((length, PAIR), lambda p: (0, 0))
    column = pl.BlockSpec((length, 1), lambda p: (0, 0))
    return pl.pallas_call(
        partial(attend_back_kernel, math.sqrt(HEAD)),
        grid=(pairs,),
        in_specs=[
            pair_spec(length, first), pair_spec(length, first + every), pair_spec(length, first + 2 * every),
            pair_spec(length, first), pair_spec(length, first + base),
            whole, whole, pl.BlockSpec((1, PAIR), lambda p: (0, p + first + base)), column, pair_spec(length, first),
        ],
        out_specs=[
            pl.BlockSpec((3, length, PAIR), lambda p: (0, 0, p)),
            pl.BlockSpec((1, 8, PAIR), lambda p: (p, 0, 0)),
        ],
        scratch_shapes=[pltpu.VMEM((2, length, PAIR), jnp.bfloat16)] * 4
        + [pltpu.VMEM((length, PAIR), jnp.float32)]
        + [pltpu.VMEM((2, length, PAIR), jnp.float32)] * 2,
        out_shape=[
            far_array((3, length, pairs * PAIR), jnp.bfloat16),
            jax.ShapeDtypeStruct((pairs, 8, PAIR), jnp.float32),
        ],
        compiler_params=pltpu.CompilerParams(vmem_limit_bytes=48 << 20),
        cost_estimate=pl.CostEstimate(
            flops=60 * length * length * pairs * PAIR, bytes_accessed=18 * length * pairs * PAIR,
            transcendentals=length * length * pairs * 2,
        ),
        name="attend_back",
    )(far(qkv), far(qkv), far(qkv), far(out), far(grad), far(cosine), far(sine), scale, far(segs), far(lse))


def rotary_wide(positions):
    half = HEAD // 2
    freq = jnp.power(10000.0, -2.0 * jnp.arange(half, dtype=jnp.float32) / HEAD)
    angle = positions.astype(jnp.float32)[:, None] * freq
    cosine = jnp.cos(angle)
    sine = jnp.sin(angle)
    return (
        jnp.concatenate([cosine] * 4, axis=1),
        jnp.concatenate([-sine, sine, -sine, sine], axis=1),
    )


def far_array(shape, kind):
    return pltpu.HBM(shape, kind)


def far(value):
    return pltpu.with_memory_space_constraint(value, pltpu.HBM)


def mean_last(value):
    return jnp.mean(value, axis=-1, keepdims=True)


def sort_matrix(core, each):
    left = lax.broadcasted_iota(jnp.int32, (256, 256), 0)
    right = lax.broadcasted_iota(jnp.int32, (256, 256), 1)
    place = right % 128
    source = (place // each * 2 + (core + 1 + right // 128) % 2) * each + place % each
    return (left == source).astype(jnp.bfloat16)


def sort_cores(value, matrix, out_ref, start):
    half = out_ref.shape[1] // 2
    for n in range(value.shape[1] // 256):
        both = jnp.dot(value[:, 256 * n : 256 * (n + 1)], matrix, preferred_element_type=jnp.float32)
        at = start + 128 * n
        out_ref[:, at : at + 128] = both[:, :128].astype(jnp.bfloat16)
        out_ref[:, half + at : half + at + 128] = both[:, 128:].astype(jnp.bfloat16)


def sort_kernel(each, core_ref, value_ref, out_ref):
    sort_cores(value_ref[...], sort_matrix(core_ref[0], each), out_ref, 0)


def sorted_cores(value, core, each):
    rows, width = value.shape
    tile = min(512, rows)
    spec = pl.BlockSpec((tile, width), lambda i: (i, 0))
    return pl.pallas_call(
        partial(sort_kernel, each),
        grid=(rows // tile,),
        in_specs=[pl.BlockSpec(memory_space=pltpu.SMEM), spec],
        out_specs=spec,
        out_shape=jax.ShapeDtypeStruct((rows, width), value.dtype),
        cost_estimate=pl.CostEstimate(flops=512 * rows * width, bytes_accessed=4 * rows * width, transcendentals=0),
        name="sort_cores",
    )(core, value)


def after_attention_kernel(each, core_ref, a0_ref, a1_ref, w_ref, x_ref, alpha_ref,
                           branch_ref, h_ref, low_ref, hs_ref):
    f32 = jnp.float32
    half = a0_ref.shape[1]
    matrix = sort_matrix(core_ref[0], each)
    branch = jnp.dot(a0_ref[...], w_ref[:half, :], preferred_element_type=f32)
    branch = branch + jnp.dot(a1_ref[...], w_ref[half:, :], preferred_element_type=f32)
    branch_ref[...] = branch
    unit = branch * lax.rsqrt(mean_last(branch * branch) + EPS)
    x = x_ref[...].astype(f32)
    z = x + alpha_ref[...] * (unit - x)
    h = z * lax.rsqrt(mean_last(z * z) + EPS)
    low = h.astype(jnp.bfloat16)
    h_ref[...] = h
    low_ref[...] = low
    sort_cores(low, matrix, hs_ref, 0)


def after_attention(core, each, att, w_out, tokens, alpha):
    rows, width = tokens.shape
    tile = min(512, rows)
    full = pl.BlockSpec((tile, width), lambda i: (i, 0))
    half = pl.BlockSpec((tile, width // 2), lambda i: (i, 0))
    shape = lambda cols, kind: jax.ShapeDtypeStruct((rows, cols), kind)
    return pl.pallas_call(
        partial(after_attention_kernel, each),
        grid=(rows // tile,),
        in_specs=[
            pl.BlockSpec(memory_space=pltpu.SMEM), half, half,
            pl.BlockSpec((width, width), lambda i: (0, 0)), full, pl.BlockSpec((1, width), lambda i: (0, 0)),
        ],
        out_specs=[full] * 4,
        out_shape=[shape(width, jnp.float32)] * 2 + [shape(width, jnp.bfloat16)] * 2,
        compiler_params=pltpu.CompilerParams(vmem_limit_bytes=40 << 20),
        cost_estimate=pl.CostEstimate(flops=2 * rows * width * width, bytes_accessed=20 * rows * width, transcendentals=0),
        name="after_attention",
    )(core, *att, w_out, tokens, alpha)


def sigmoid(value):
    return 0.5 * jnp.tanh(0.5 * value) + 0.5


def up_kernel(h_ref, wu_ref, wg_ref, su_ref, sg_ref, *refs):
    f32 = jnp.float32
    bf16 = jnp.bfloat16
    up_ref, gate_ref, hid_ref = refs[-3:]
    up = jnp.dot(h_ref[...], wu_ref[...], preferred_element_type=f32)
    gate = jnp.dot(h_ref[...], wg_ref[...], preferred_element_type=f32)
    value = gate * sg_ref[...]
    up_ref[...] = up.astype(bf16)
    gate_ref[...] = gate.astype(bf16)
    hid_ref[...] = (up * su_ref[...] * (value * sigmoid(value))).astype(bf16)


def feed_up(part, parts, h_low, w, scale_up, scale_gate, before):
    rows, width = h_low.shape
    ff = scale_up.shape[1]
    q = w.shape[1] // 2
    block = min(512, q)
    steps = q // block
    first = part * steps
    out = pl.BlockSpec((rows, block), lambda j: (0, first + j))
    line = pl.BlockSpec((1, block), lambda j: (0, first + j))
    shape = far_array((rows, ff), jnp.bfloat16)
    return pl.pallas_call(
        up_kernel,
        grid=(steps,),
        in_specs=[
            pl.BlockSpec((rows, width), lambda j: (0, 0)),
            pl.BlockSpec((width, block), lambda j: (0, j)),
            pl.BlockSpec((width, block), lambda j: (0, steps + j)),
            line, line,
        ] + [pl.BlockSpec(memory_space=pl.ANY)] * len(before),
        out_specs=[out] * 3,
        out_shape=[shape] * 3,
        input_output_aliases={5 + n: n for n in range(len(before))},
        compiler_params=pltpu.CompilerParams(vmem_limit_bytes=48 << 20),
        cost_estimate=pl.CostEstimate(flops=4 * rows * width * q, bytes_accessed=2 * (rows * width + 2 * width * q + 3 * rows * q), transcendentals=rows * q),
        name="feed_up",
    )(h_low, w, w, scale_up, scale_gate, *before)


def finish_kernel(steps, hid_ref, w0_ref, w1_ref, h1_ref, t_ref, mask_ref, alpha_ref,
                  out_ref, gm_ref, gz_ref, ga_ref, loss_ref, acc):
    f32 = jnp.float32
    bf16 = jnp.bfloat16
    step = pl.program_id(0)
    half = w0_ref.shape[1]

    @pl.when(step == 0)
    def _():
        acc[...] = jnp.zeros_like(acc)

    acc[:, :half] += jnp.dot(hid_ref[...], w0_ref[...], preferred_element_type=f32)
    acc[:, half:] += jnp.dot(hid_ref[...], w1_ref[...], preferred_element_type=f32)

    @pl.when(step == steps - 1)
    def _():
        alpha = alpha_ref[...]
        grads = jnp.zeros(ga_ref.shape, f32)
        losses = jnp.zeros(loss_ref.shape, f32)
        tile = min(256, acc.shape[0])
        for at in range(0, acc.shape[0], tile):
            rows = pl.ds(at, tile)
            branch = acc[rows, :]
            factor = lax.rsqrt(mean_last(branch * branch) + EPS)
            unit = branch * factor
            h1 = h1_ref[rows, :]
            z = h1 + alpha * (unit - h1)
            z_factor = lax.rsqrt(mean_last(z * z) + EPS)
            h2 = z * z_factor
            out_ref[rows, :] = h2.astype(bf16)
            diff = h2 - t_ref[rows, :].astype(f32)
            masked = mask_ref[rows, :] * diff
            grad = 2.0 * masked
            gz = z_factor * (grad - h2 * mean_last(grad * h2))
            gz_ref[rows, :] = (1.0 - alpha) * gz
            back = alpha * gz
            gm_ref[rows, :] = (factor * (back - unit * mean_last(back * unit))).astype(bf16)
            grads = grads + jnp.sum(gz * (unit - h1), axis=0, keepdims=True)
            losses = losses + jnp.sum(masked * diff, axis=0, keepdims=True)
        ga_ref[...] = grads
        loss_ref[...] = losses


def finish(hidden, down, h1, teacher, mask, alpha):
    rows, ff = hidden.shape
    width = h1.shape[1]
    block = min(1024, ff)
    steps = ff // block
    once = pl.Buffered(1)
    whole = lambda cols=width: pl.BlockSpec((rows, cols), lambda j: (0, 0), pipeline_mode=once)
    row = pl.BlockSpec((1, width), lambda j: (0, 0))
    deep = pl.BlockSpec((block, width // 2), lambda j: (j, 0))
    line = jax.ShapeDtypeStruct((1, width), jnp.float32)
    return pl.pallas_call(
        partial(finish_kernel, steps),
        grid=(steps,),
        in_specs=[
            pl.BlockSpec((rows, block), lambda j: (0, j)),
            deep, deep, whole(), whole(), whole(1), row,
        ],
        out_specs=[whole(), whole(), whole(), row, row],
        out_shape=[
            far_array((rows, width), jnp.bfloat16), jax.ShapeDtypeStruct((rows, width), jnp.bfloat16),
            far_array((rows, width), jnp.float32), line, line,
        ],
        scratch_shapes=[pltpu.VMEM((rows, width), jnp.float32)],
        compiler_params=pltpu.CompilerParams(vmem_limit_bytes=48 << 20),
        cost_estimate=pl.CostEstimate(flops=2 * rows * width * ff, bytes_accessed=2 * (rows + width) * ff + 16 * rows * width, transcendentals=0),
        name="finish",
    )(hidden, *down, h1, teacher, mask, alpha)


def feed_back_kernel(steps, each, last, g_ref, left_ref, w0_ref, w1_ref, up_ref, gate_ref, su_ref, sg_ref, wu_ref, wg_ref, start_ref, *refs):
    f32 = jnp.float32
    bf16 = jnp.bfloat16
    step = pl.program_id(0)
    half = w0_ref.shape[1]
    if last:
        branch_ref, x_ref, alpha_ref, gsu_ref, gsg_ref, other_ref, own_ref, gb_ref, gx_ref, ga_ref, acc = refs
        parts = (other_ref, own_ref)
    else:
        gsu_ref, gsg_ref, all_ref, acc = refs
        parts = (all_ref,)

    @pl.when(step == 0)
    def _():
        acc[...] = start_ref[...]

    su = su_ref[...]
    sg = sg_ref[...]
    back = dot_last(g_ref[:, :half], w0_ref[...]) + dot_last(g_ref[:, half:], w1_ref[...])
    up = up_ref[...].astype(f32)
    gate = gate_ref[...].astype(f32)
    value = gate * sg
    sig = sigmoid(value)
    active = value * sig
    with_active = back * active
    g_value = back * up * su * (sig + active * (1.0 - sig))
    g_up = (with_active * su).astype(bf16)
    g_gate = (g_value * sg).astype(bf16)
    gsu_ref[...] = jnp.sum(with_active * up, axis=0, keepdims=True)
    gsg_ref[...] = jnp.sum(g_value * gate, axis=0, keepdims=True)
    acc[...] += dot_last(g_up, wu_ref[...])
    acc[...] += dot_last(g_gate, wg_ref[...])
    for n, grad in enumerate((g_up, g_gate)):
        rows = dot_first(left_ref[...], grad).astype(bf16)
        at = 0
        for part in parts:
            for group in range(part.shape[0]):
                part[group, n] = rows[at : at + each, :]
                at += each
    if not last:
        return

    @pl.when(step == steps - 1)
    def _():
        alpha = alpha_ref[...]
        tile = min(256, acc.shape[0])
        total = jnp.zeros(ga_ref.shape, f32)
        for at in range(0, acc.shape[0], tile):
            branch = branch_ref[at : at + tile, :]
            a_factor = lax.rsqrt(mean_last(branch * branch) + EPS)
            unit = branch * a_factor
            x = x_ref[at : at + tile, :].astype(f32)
            z = x + alpha * (unit - x)
            z_factor = lax.rsqrt(mean_last(z * z) + EPS)
            h = z * z_factor
            grad = acc[at : at + tile, :]
            gz = z_factor * (grad - h * mean_last(grad * h))
            total = total + jnp.sum(gz * (unit - x), axis=0, keepdims=True)
            back = alpha * gz
            gb_ref[at : at + tile, :] = (a_factor * (back - unit * mean_last(back * unit))).astype(bf16)
            gx_ref[at : at + tile, :] = (1.0 - alpha) * gz
        ga_ref[...] = total


def feed_back(part, parts, shards, g, left, down, up, gate, scale_up, scale_gate, w, start, rest=None):
    rows, width = g.shape
    ff = up.shape[1]
    block = min(512, ff // parts)
    steps = ff // parts // block
    first = part * steps
    each = width // shards
    last = rest is not None
    once = pl.Buffered(1)
    whole = lambda: pl.BlockSpec((rows, width), lambda j: (0, 0), pipeline_mode=once)
    col = pl.BlockSpec((rows, block), lambda j: (0, first + j))
    line = pl.BlockSpec((1, block), lambda j: (0, first + j))
    sums = pl.BlockSpec((1, block), lambda j: (0, j))
    row = pl.BlockSpec((1, width), lambda j: (0, 0))
    deep = pl.BlockSpec((block, width // 2), lambda j: (first + j, 0))
    small = jax.ShapeDtypeStruct((1, ff // parts), jnp.float32)
    specs = [
        whole(), whole(), deep, deep, col, col, line, line,
        pl.BlockSpec((width, block), lambda j: (0, j)),
        pl.BlockSpec((width, block), lambda j: (0, steps + j)),
        whole(),
    ]
    operands = [g, left, *down, up, gate, scale_up, scale_gate, w, w, start]
    groups = shards // 2 if last else shards
    grads = pl.BlockSpec((groups, 2, each, block), lambda j: (0, 0, 0, j))
    shape = far_array((groups, 2, each, ff // parts), jnp.bfloat16)
    full = jax.ShapeDtypeStruct((rows, width), jnp.float32)
    scratch = []
    if last:
        specs += [whole(), whole(), row]
        operands += rest
        out_specs = [sums, sums, grads, grads, whole(), whole(), row]
        out_shape = [small, small, shape, shape, jax.ShapeDtypeStruct((rows, width), jnp.bfloat16), far_array((rows, width), jnp.float32),
                     jax.ShapeDtypeStruct((1, width), jnp.float32)]
        scratch = [pltpu.VMEM((rows, width), jnp.float32)]
    else:
        out_specs = [sums, sums, grads, pl.BlockSpec((rows, width), lambda j: (0, 0), pipeline_mode=once)]
        out_shape = [small, small, shape, full]
    return pl.pallas_call(
        partial(feed_back_kernel, steps, each, last),
        grid=(steps,),
        in_specs=specs,
        out_specs=out_specs,
        out_shape=out_shape,
        scratch_shapes=scratch,
        compiler_params=pltpu.CompilerParams(vmem_limit_bytes=61 << 20),
        cost_estimate=pl.CostEstimate(flops=10 * rows * width * ff // parts, bytes_accessed=10 * (rows + width) * ff // parts + 16 * rows * width, transcendentals=rows * ff // parts),
        name="feed_back",
    )(*operands)


def down_grad_kernel(each, core_ref, h_ref, g_ref, other_ref, own_ref, whole_ref):
    whole_ref[...] = dot_first(h_ref[...], g_ref[...])
    core = core_ref[0]
    for n in range(h_ref.shape[1] // (2 * each)):
        for out_ref, which in ((other_ref, 1 - core), (own_ref, core)):
            start = pl.multiple_of((2 * n + which) * each, each)
            out_ref[n * each : (n + 1) * each, :] = whole_ref[pl.ds(start, each), :].astype(jnp.bfloat16)


def down_grad(core, hidden, g, groups):
    rows, ff = hidden.shape
    width = g.shape[1]
    each = ff // (2 * groups)
    block = min(1024, ff)
    out = pl.BlockSpec((block // 2, width), lambda i: (i, 0))
    shape = far_array((ff // 2, width), jnp.bfloat16)
    return pl.pallas_call(
        partial(down_grad_kernel, each),
        grid=(ff // block,),
        in_specs=[
            pl.BlockSpec(memory_space=pltpu.SMEM),
            pl.BlockSpec((rows, block), lambda i: (0, i)),
            pl.BlockSpec((rows, width), lambda i: (0, 0)),
        ],
        out_specs=[out, out],
        out_shape=[shape, shape],
        scratch_shapes=[pltpu.VMEM((block, width), jnp.float32)],
        compiler_params=pltpu.CompilerParams(vmem_limit_bytes=40 << 20),
        cost_estimate=pl.CostEstimate(flops=2 * rows * ff * width, bytes_accessed=2 * rows * ff + 2 * ff * width + 2 * rows * width, transcendentals=0),
        name="down_grad",
    )(core, hidden, g)


def row_grad_kernel(left_ref, *refs):
    rights, (other_ref, own_ref) = refs[:-2], refs[-2:]
    half = other_ref.shape[0]
    at = 0
    for right in rights:
        cols = right.shape[1]
        both = dot_first(left_ref[...], right[...])
        other_ref[:, at : at + cols] = both[:half, :].astype(jnp.bfloat16)
        own_ref[:, at : at + cols] = both[half:, :].astype(jnp.bfloat16)
        at += cols


def rows_kernel(count, *refs):
    lefts, rights, out_ref = refs[:count], refs[count:-1], refs[-1]
    at = 0
    for left in lefts:
        row = left.shape[1]
        col = 0
        for right in rights:
            cols = right.shape[1]
            out_ref[at : at + row, col : col + cols] = dot_first(left[...], right[...]).astype(jnp.bfloat16)
            col += cols
        at += row


def out_grad(lefts, right, total):
    rows, width = right.shape
    every = sum(left.shape[1] for left in lefts)
    block = min(512, width)
    return pl.pallas_call(
        partial(rows_kernel, len(lefts)),
        grid=(width // block,),
        in_specs=[pl.BlockSpec(left.shape, lambda j: (0, 0)) for left in lefts]
        + [pl.BlockSpec((rows, block), lambda j: (0, j))],
        out_specs=pl.BlockSpec((every, block), lambda j: (0, j)),
        out_shape=far_array((every, total), jnp.bfloat16),
        compiler_params=pltpu.CompilerParams(vmem_limit_bytes=40 << 20),
        cost_estimate=pl.CostEstimate(flops=2 * rows * width * every, bytes_accessed=2 * (rows * (width + every) + width * every), transcendentals=0),
        name="out_grad",
    )(*lefts, right)


def heads_grad(left, parts, before=None, wide=0):
    rows, width = left.shape
    cols = parts[0].shape[2]
    count = len(parts)
    each = cols * count
    lefts = pl.BlockSpec((rows, width), lambda j: (0, 0))
    rights = [pl.BlockSpec((pl.Squeezed(), rows, cols), lambda j: (j, 0, 0))] * count
    params = dict(
        compiler_params=pltpu.CompilerParams(vmem_limit_bytes=40 << 20),
        cost_estimate=pl.CostEstimate(flops=6 * rows * width * each, bytes_accessed=2 * (rows * width + 3 * (width + rows) * each), transcendentals=0),
        name="heads_grad",
    )
    if before is None:
        out = pl.BlockSpec((width // 2, each), lambda j: (0, j))
        shape = far_array((width // 2, 3 * each + wide), jnp.bfloat16)
        return pl.pallas_call(
            row_grad_kernel, grid=(3,), in_specs=[lefts] + rights, out_specs=[out, out], out_shape=[shape, shape], **params
        )(left, *parts)
    first = before.shape[1] // each - 3
    return pl.pallas_call(
        rows_under_kernel,
        grid=(3,),
        in_specs=[lefts] + rights + [pl.BlockSpec(memory_space=pl.ANY)],
        out_specs=pl.BlockSpec((width, each), lambda j: (0, first + j)),
        out_shape=far_array(before.shape, jnp.bfloat16),
        input_output_aliases={1 + count: 0},
        **params,
    )(left, *parts, before)


def rows_under_kernel(left_ref, *refs):
    rows_kernel(1, left_ref, *refs[:-2], refs[-1])


def input_grad_kernel(scale_ref, base_ref, *refs):
    out_ref = refs[-1]
    count = len(refs) // 3
    total = base_ref[...]
    for n in range(count):
        first, second, w = refs[n * 3 : n * 3 + 3]
        cols = first.shape[2]
        for p in range(3):
            at = 2 * p * cols
            total = total + dot_last(first[p], w[:, at : at + cols])
            total = total + dot_last(second[p], w[:, at + cols : at + 2 * cols])
    out_ref[...] = total * scale_ref[0]


def input_grad(scale, base, parts, weights):
    rows, width = base.shape
    tile = min(256, width)
    out = pl.BlockSpec((rows, tile), lambda j: (0, j))
    specs, operands = [], []
    for n, w in enumerate(weights):
        for part in parts[2 * n : 2 * n + 2]:
            specs.append(pl.BlockSpec(part.shape, lambda j: (0, 0, 0), pipeline_mode=pl.Buffered(1)))
            operands.append(part)
        specs.append(pl.BlockSpec((tile, w.shape[1]), lambda j: (j, 0)))
        operands.append(w)
    flops = 2 * rows * width * sum(w.shape[1] for w in weights)
    return pl.pallas_call(
        input_grad_kernel,
        grid=(width // tile,),
        in_specs=[pl.BlockSpec(memory_space=pltpu.SMEM), out] + specs,
        out_specs=out,
        out_shape=jax.ShapeDtypeStruct((rows, width), jnp.float32),
        compiler_params=pltpu.CompilerParams(vmem_limit_bytes=48 << 20),
        cost_estimate=pl.CostEstimate(flops=flops, bytes_accessed=20 * rows * width, transcendentals=0),
        name="input_grad",
    )(scale, base, *operands)


def slots_kernel(plan, rows, extras, slots, keep, got, *refs):
    f32 = jnp.float32
    terms = refs[:extras]
    outs = refs[extras : extras + len(plan)]
    kept, gotten, sems = refs[extras + len(plan) :]
    total = sum(len(blocks) for blocks in plan)
    copies = []
    for b in range(total):
        place = pl.ds(pl.multiple_of(slots[b] * rows, rows), rows)
        pair = (
            pltpu.make_async_copy(keep.at[place], kept.at[b], sems.at[0, b]),
            pltpu.make_async_copy(got.at[place], gotten.at[b], sems.at[1, b]),
        )
        for copy in pair:
            copy.start()
        copies.append(pair)
    b = 0
    for out, blocks in zip(outs, plan):
        for n, uses in enumerate(blocks):
            for copy in copies[b]:
                copy.wait()
            value = kept[b].astype(f32) + gotten[b].astype(f32)
            for term, at in uses:
                value = value + terms[term][at * rows : (at + 1) * rows, :].astype(f32)
            out[n * rows : (n + 1) * rows, :] = value.astype(out.dtype)
            b += 1


def add_slots(keep, got, rows, slots, plan, terms=()):
    cols = keep.shape[1]
    total = len(slots)
    vmem = pl.BlockSpec(memory_space=pltpu.VMEM)
    block = rows * cols
    return pl.pallas_call(
        partial(slots_kernel, plan, rows, len(terms)),
        in_specs=[pl.BlockSpec(memory_space=pltpu.SMEM)] + [pl.BlockSpec(memory_space=pl.ANY)] * 2 + [vmem] * len(terms),
        out_specs=[vmem] * len(plan),
        out_shape=[jax.ShapeDtypeStruct((len(blocks) * rows, cols), keep.dtype) for blocks in plan],
        scratch_shapes=[
            pltpu.VMEM((total, rows, cols), keep.dtype),
            pltpu.VMEM((total, rows, cols), keep.dtype),
            pltpu.SemaphoreType.DMA((2, total)),
        ],
        compiler_params=pltpu.CompilerParams(vmem_limit_bytes=8 * total * block + 8 * block + (4 << 20)),
        cost_estimate=pl.CostEstimate(flops=0, bytes_accessed=8 * total * block, transcendentals=0),
        name="add_slots",
    )(jnp.stack(slots).astype(jnp.int32), far(keep), far(got), *terms)


def body(
    tokens,
    teacher,
    valid,
    segments,
    positions,
    w_qkv,
    w_out,
    w_upgate,
    w_down,
    s_qk,
    alpha_attn,
    s_up,
    s_gate,
    alpha_mlp,
):
    f32 = jnp.float32
    bf16 = jnp.bfloat16
    at = Place()
    rows, width = tokens.shape
    ff = w_upgate.shape[1] // 2
    each = w_out.shape[0]
    groups = at.shards // NC
    core = at.core.reshape(1).astype(jnp.int32)
    half = width // 2
    pairs = half // PAIR
    segs = segments.reshape(rows, 1)

    def columns(w, starts, size):
        return jnp.concatenate([w[:, s : s + size] for s in starts], axis=1)

    chunks = [columns(w_qkv, [p * width + n * half for p in range(3)], half) for n in range(2)]
    vectors = (s_qk, alpha_attn, s_up, s_gate, alpha_mlp)
    short = jnp.concatenate(vectors).reshape(each, -1)
    per_row = short.shape[1]
    chunks[0] = jnp.concatenate([chunks[0], jnp.pad(short, ((0, 0), (0, PAIR - per_row)))], axis=1)
    chunks.append(w_out)
    chunks += [w_down[:, :half], w_down[:, half:]]

    gather = Gather(at, chunks[:3])
    late = Gather(at, chunks[3:])
    mask = valid.astype(f32)
    upgate = [
        lax.all_gather(columns(w_upgate, [n * ff // 2, ff + n * ff // 2], ff // 2), "shard", axis=0, tiled=True)
        for n in range(2)
    ]
    gate = []
    for tick in range(4):
        moved = gather.tick(tick, gate)
        if tick == 3:
            late.tick(0, gate)
        if tick == 0:
            cosine, sine = rotary_wide(positions.reshape(rows))
            moved += [cosine, sine]
        if tick == 1:
            x_sorted = sorted_cores(after(tokens, gate + gather.sends), core, each)
            moved += [x_sorted]
        gate = moved
    def dot(left, right):
        return jnp.dot(left, right, preferred_element_type=f32).astype(bf16)

    weights, qkv, att, lse = {}, [], [], []
    for n in range(2):
        moved = gather.tick(4 + n, gate)
        late.tick(1 + n, gate)
        gate = gate + gather.sends
        weights[n] = gather.full(n)
        if n == 0:
            found = weights[0][:, 3 * half : 3 * half + per_row].astype(f32).reshape(at.shards, -1)
            shorts, place = [], 0
            for vector in vectors:
                size = vector.shape[0]
                shorts.append(found[:, place : place + size].reshape(1, -1))
                place += size
            f_sqk, f_aa, f_su, f_sg, f_am = shorts
        qkv.append(dot(after(tokens, gate), weights[n][:, : 3 * half]))
        out, sums = attention(qkv[n], cosine, sine, f_sqk, segs, n * half)
        att.append(out)
        lse.append(sums)
        gate = moved + [out]
    late.tick(3, gate)
    weights[2] = gather.full(2)
    att = [after(a, gate) for a in att]
    branch_a, h_one, h_low, h_sorted = after_attention(
        core, each, [far(a) for a in att], weights[2], tokens, f_aa
    )
    before = feed_up(0, 2, h_low, upgate[0], f_su, f_sg, [])
    late.tick(4, [before[2]])
    before = feed_up(1, 2, after(h_low, [before[2]]), upgate[1], f_su, f_sg, before)
    down = [late.full(0), late.full(1)]
    up, gate_part, hidden = before
    output, g_bm, gz, grad_am, loss_rows = finish(
        hidden, down, h_one, teacher, mask.reshape(rows, 1), f_am
    )

    waiting = {}

    def window(gate, names, late=()):
        moved = []
        sends = list(gate)
        for name in names:
            moved += waiting[name].step(gate)
            sends += waiting[name].sends
        for name in late:
            waiting[name].step(gate)
            sends += waiting[name].sends
        return moved, sends

    upper = lax.broadcasted_iota(jnp.int32, (8, 128), 0) < 4
    counted = Sum(at, jnp.where(upper, jnp.sum(loss_rows), jnp.sum(mask)))
    waiting["down"] = Reduce(at, *down_grad(core, hidden, g_bm, groups))
    gate = [waiting["down"].send, waiting["down"].keep]
    moved, gate = window(gate, ["down"])
    moved += counted.step(gate)
    su0, sg0, first_up, acc = feed_back(
        0, 2, at.shards, after(g_bm, gate), h_low, down, up, gate_part, f_su, f_sg, upgate[0], gz
    )
    gate = moved + [acc]
    moved, gate = window(gate, ["down"])
    moved += counted.step(gate)
    first_up = lax.psum_scatter(after(first_up, gate), "shard", scatter_dimension=0, tiled=True)
    su1, sg1, up_other, up_own, g_ba, gx_base, grad_aa = feed_back(
        1, 2, at.shards, after(g_bm, gate), h_sorted, down, up, gate_part, f_su, f_sg, upgate[1], acc,
        [branch_a, tokens, f_aa],
    )
    waiting["up"] = Reduce(at, up_other.reshape(width, ff // 2), up_own.reshape(width, ff // 2))
    gate = moved + [g_ba]

    g3, g_scale = {}, []

    def back(n, gate):
        part = pairs // 2
        out, sums = attention_back(
            qkv[n // 2], att[n // 2], after(g_att, gate), lse[n // 2], cosine, sine, f_sqk, segs,
            n // 2 * half, n % 2 * part, part,
        )
        g3[n] = out
        g_scale.append(sums[:, 0, :].reshape(-1))
        return [out]

    moved, gate = window(gate, ["up"], ["down"])
    moved += counted.step(gate)
    g_att = lax.dot_general(
        after(g_ba, gate), weights[2], (((1,), (1,)), ((), ())), preferred_element_type=f32
    ).astype(bf16)
    attended = out_grad(att, after(g_ba, gate), width + 3 * half)
    gate = moved + [g_att]
    moved, gate = window(gate, ["up"])
    moved += counted.step(gate)
    back(0, gate)
    gate = moved + back(1, [g3[0]])
    over_x, gate = window(gate, ["up"])
    over_x += counted.step(gate)
    attended = heads_grad(after(tokens, gate), [g3[0], g3[1]], attended)
    own_att = lax.psum_scatter(attended, "shard", scatter_dimension=0, tiled=True)
    moved, gate = window([attended], ["down"])
    back(2, gate)
    first_up = after(first_up.reshape(2 * each, ff // 2), [g3[2]])
    last_up = at.along_y(first_up)
    gate = moved + over_x + back(3, [g3[2]])
    counts = counted.total()
    count = jnp.maximum(counts[4, 0], 1.0)
    loss = counts[0, 0] / count
    scale = rows * at.reps * at.shards / count
    over_z, gate = window(gate, ["up"])
    sides = heads_grad(after(x_sorted, gate), [g3[2], g3[3]], wide=PAIR)
    shorts = [
        jnp.concatenate(g_scale), grad_aa.reshape(-1), jnp.concatenate([su0, su1], axis=1).reshape(-1),
        jnp.concatenate([sg0, sg1], axis=1).reshape(-1), grad_am.reshape(-1),
    ]
    shorts = jnp.concatenate([s.reshape(at.shards, -1) for s in shorts], axis=1).astype(bf16)
    shorts = jnp.pad(shorts.reshape(groups, NC, each, per_row), ((0, 0), (0, 0), (0, 0), (0, PAIR - per_row)))
    sides = [
        lax.dynamic_update_slice(
            side, lax.dynamic_index_in_dim(shorts, which, axis=1, keepdims=False).reshape(-1, PAIR), (0, 3 * half)
        )
        for side, which in zip(sides, (1 - at.core, at.core))
    ]
    waiting["qkv1"] = Reduce(at, *sides)
    gate = list(sides) + [last_up]
    gate, _ = window(gate, ["qkv1"])
    gate, _ = window(gate, ["qkv1"])
    moved, sends = window(gate, ["qkv1"])
    last_down, _ = window(gate, ["down"])
    moved += last_down
    grad_x = input_grad(
        scale.reshape(1), after(gx_base, sends), [g3[n] for n in range(4)], [weights[0], weights[1]]
    )
    gate = moved + over_z + [grad_x]
    gate, _ = window(gate, ["qkv1", "up"])
    own_att = after(own_att, gate)
    last_att = at.along_y(own_att)
    window(gate, ["qkv1"])
    total = {name: chunk.total() * scale for name, chunk in waiting.items()}

    def whole(mine, other):
        return over_copies(at, mine.astype(f32) + other.astype(f32), 2) * scale

    attended = whole(own_att, last_att)
    q0, q1 = (jnp.split(v, 3, axis=1) for v in (attended[:, width:], total["qkv1"][:, : 3 * half]))
    shorts = total["qkv1"][:, 3 * half : 3 * half + per_row].reshape(-1)
    owned, place = [], 0
    for vector in vectors:
        owned.append(shorts[place : place + vector.shape[0]])
        place += vector.shape[0]
    own_qkv = jnp.concatenate([part for two in zip(q0, q1) for part in two], axis=1)
    first_up = whole(first_up, last_up)
    ups = [first_up[:each], total["up"][:each], first_up[each:], total["up"][each:]]
    own_up = jnp.concatenate(ups, axis=1)
    return (output, loss, grad_x, own_qkv, attended[:, :width], own_up, total["down"], *owned)


def solution(mesh):
    return jax.shard_map(
        body,
        mesh=mesh,
        in_specs=(
            P(("rep", "shard"), None),
            P(("rep", "shard"), None),
            P(("rep", "shard")),
            P(("rep", "shard"), None),
            P(("rep", "shard"), None),
            P("shard", None),
            P("shard", None),
            P("shard", None),
            P("shard", None),
            P("shard"),
            P("shard"),
            P("shard"),
            P("shard"),
            P("shard"),
        ),
        out_specs=(
            P(("rep", "shard"), None),
            P(),
            P(("rep", "shard"), None),
            P("shard", None),
            P("shard", None),
            P("shard", None),
            P("shard", None),
            P("shard"),
            P("shard"),
            P("shard"),
            P("shard"),
            P("shard"),
        ),
        check_vma=False,
    )
```

```python
from functools import partial
import math

import jax
import jax.numpy as jnp
from jax import lax
from jax.experimental import pallas as pl
from jax.experimental.pallas import tpu as pltpu
from jax.sharding import PartitionSpec as P

EPS = 1e-06
AXES = ("rep", "shard")
NZ = 4
NC = 2


class Place:
    def __init__(self):
        self.reps = lax.axis_size("rep")
        self.shards = lax.axis_size("shard")
        self.nx = self.shards // (NZ * NC)
        self.pairs = self.reps % 2 == 0
        rep = lax.axis_index("rep")
        shard = lax.axis_index("shard")
        self.rep = rep
        self.shard = shard
        self.y = rep % 2
        self.core = shard % NC
        self.x = (shard // NC) % self.nx
        self.z = shard // (NC * self.nx)

    def moves(self, step):
        pairs = []
        for rep in range(self.reps):
            for z in range(NZ):
                for x in range(self.nx):
                    for core in range(NC):
                        to_rep, to_z, to_x, to_core = step(rep, z, x, core)
                        pairs.append(
                            (
                                rep * self.shards + (z * self.nx + x) * NC + core,
                                to_rep * self.shards + (to_z * self.nx + to_x) * NC + to_core,
                            )
                        )
        return pairs

    def near_z(self, value):
        return lax.ppermute(value, AXES, self.moves(lambda r, z, x, c: (r, z ^ 1, x, c)))

    def far_z(self, value):
        return lax.ppermute(value, AXES, self.moves(lambda r, z, x, c: (r, z ^ (2 + r % 2), x, c)))

    def along_x(self, value, j):
        return lax.ppermute(value, AXES, self.moves(lambda r, z, x, c: (r, z, x ^ j, c)))

    def along_y(self, value):
        return lax.ppermute(value, AXES, self.moves(lambda r, z, x, c: (r ^ 1, z, x, c)))

    def other_core(self, value):
        return lax.ppermute(value, AXES, self.moves(lambda r, z, x, c: (r, z, x, c ^ 1)))

    def flat(self, value, bit):
        count = self.reps * self.shards
        return lax.ppermute(value, AXES, [(i, i ^ bit) for i in range(count)])

    def slot(self, k, j):
        return (self.z ^ k) * self.nx + (self.x ^ j)


def tie(*values):
    return lax.optimization_barrier(values)


def place_kernel(count, slots, *refs):
    pieces, out = refs[:-1], refs[-1]
    for i in range(count):
        rows = pieces[i].shape[0]
        at = pl.multiple_of(slots[i] * rows, rows)
        out[pl.ds(at, rows), :] = pieces[i][...]


def assemble(pieces, slots, rows_out):
    cols = pieces[0].shape[1]
    size = rows_out * cols * pieces[0].dtype.itemsize
    return pl.pallas_call(
        partial(place_kernel, len(pieces)),
        out_shape=jax.ShapeDtypeStruct((rows_out, cols), pieces[0].dtype),
        in_specs=[pl.BlockSpec(memory_space=pltpu.SMEM)]
        + [pl.BlockSpec(memory_space=pltpu.VMEM)] * len(pieces),
        out_specs=pl.BlockSpec(memory_space=pltpu.VMEM),
        compiler_params=pltpu.CompilerParams(vmem_limit_bytes=2 * size + (4 << 20)),
        cost_estimate=pl.CostEstimate(flops=0, bytes_accessed=2 * size, transcendentals=0),
    )(slots, *pieces)


def weave_kernel(columns, core, half, other, *refs):
    out, sems = refs[-2], refs[-1]
    at = core[0]
    copies = []
    for n, (source, target, size) in enumerate(columns):
        cols = pl.ds(target, size)
        copies.append(pltpu.make_async_copy(half.at[:, :, source : source + size], out.at[:, at, :, cols], sems.at[0, n]))
        copies.append(pltpu.make_async_copy(other.at[:, :, source : source + size], out.at[:, 1 - at, :, cols], sems.at[1, n]))
    for copy in copies:
        copy.start()
    for copy in copies:
        copy.wait()


def weave(half, other, core, groups, columns, total, before):
    rows, cols = half.shape
    each = rows // groups
    size = rows * cols * half.dtype.itemsize
    shape = (groups, each, cols)
    full = (groups, 2, each, total)
    return pl.pallas_call(
        partial(weave_kernel, columns),
        out_shape=jax.ShapeDtypeStruct(full, half.dtype),
        in_specs=[
            pl.BlockSpec(memory_space=pltpu.SMEM),
            pl.BlockSpec(memory_space=pltpu.VMEM),
            pl.BlockSpec(memory_space=pltpu.VMEM),
        ]
        + [pl.BlockSpec(memory_space=pl.ANY)] * len(before),
        out_specs=pl.BlockSpec(memory_space=pl.ANY),
        scratch_shapes=[pltpu.SemaphoreType.DMA((2, len(columns)))],
        input_output_aliases={3: 0} if before else {},
        compiler_params=pltpu.CompilerParams(vmem_limit_bytes=2 * size + (4 << 20)),
        cost_estimate=pl.CostEstimate(flops=0, bytes_accessed=4 * size, transcendentals=0),
        name="weave",
    )(core, half.reshape(shape), other.reshape(shape), *[b.reshape(full) for b in before]).reshape(2 * rows, total)


class Gather:
    def __init__(self, at, chunks):
        self.at = at
        self.ready = list(chunks)
        self.near, self.far, self.over_x, self.over_y = {}, {}, {}, {}
        self.own, self.other = {}, {}
        self.groups = NZ * at.nx
        self.core = at.core.reshape(1).astype(jnp.int32)

    def tick(self, tick, gate, strict=False):
        at = self.at
        count = len(self.ready)
        offsets = range(1, at.nx)
        y = at.y
        ended = []
        self.sends = []
        if tick < count:
            piece = after(self.ready[tick], gate)
            self.ready[tick] = piece
            self.near[tick] = at.near_z(piece)
            self.far[tick] = at.far_z(piece)
            ended += [self.near[tick], self.far[tick]]
        i = tick - 1
        if 0 <= i < count:
            piece = self.ready[i]
            if strict:
                self.near[i], self.far[i] = tie(self.near[i], self.far[i], *gate)[:2]
            rows = piece.shape[0]
            halves = [
                lax.dynamic_slice_in_dim(part, y * (rows // 2), rows // 2, axis=0) for part in (piece, self.near[i])
            ]
            send = after(jnp.concatenate(halves + [self.far[i]], axis=0), gate)
            self.sends.append(send)
            self.over_x[i] = [at.along_x(send, j) for j in offsets]
            ended += self.over_x[i]
        i = tick - 2
        if 0 <= i < count:
            rows = self.ready[i].shape[0]
            sends = [self.far[i]]
            sends += self.over_x[i]
            send = after(jnp.concatenate(sends, axis=0), gate)
            self.sends.append(send)
            self.over_y[i] = at.along_y(send)
            ended += [self.over_y[i]]
        i = tick - 3
        if 0 <= i < count:
            rows = self.ready[i].shape[0]
            half = rows // 2
            got = self.over_y[i]
            pieces = [self.ready[i], self.near[i], self.far[i], got[:rows]]
            slots = [at.slot(0, 0), at.slot(1, 0), at.slot(2 + y, 0), at.slot(3 - y, 0)]
            place = rows
            for mine, j in zip(self.over_x[i], offsets):
                for got_here, side in ((mine, y), (got[place : place + 2 * rows], 1 - y)):
                    pieces += [got_here[:half], got_here[half:rows], got_here[rows:]]
                    slots += [at.slot(0, j) * 2 + side, at.slot(1, j) * 2 + side, at.slot(2 + side, j)]
                place += 2 * rows
            self.own[i] = assemble(pieces, jnp.stack(slots).astype(jnp.int32), self.groups * rows)
            self.sends.append(self.own[i])
            self.other[i] = at.other_core(after(self.own[i], gate))
            ended += [self.other[i]]
        return ended

    def full(self, i, columns=None, total=None, before=()):
        cols = self.own[i].shape[1]
        columns = columns or [(0, 0, cols)]
        return weave(self.own[i], self.other[i], self.core, self.groups, columns, total or cols, before)


def after(value, gate):
    return tie(value, *gate)[0] if gate else value


class Reduce:
    def __init__(self, at, send, keep):
        self.at = at
        self.send = send
        self.keep = keep
        self.rows = keep.shape[0] // (NZ * at.nx)
        self.stage = 0

    def add(self, gate, places, plan, terms=()):
        slots = [self.at.slot(k, j) for k, j in places]
        self.sends = list(add_slots(after(self.keep, gate), self.got, self.rows, slots, plan, terms))
        return self.sends

    def step(self, gate):
        at = self.at
        offsets = range(1, at.nx)
        y = at.y
        stage = self.stage
        self.stage += 1
        if stage == 0:
            self.sends = []
            self.got = at.other_core(after(self.send, gate))
            return [self.got]
        if stage == 1:
            (send,) = self.add(gate, [(3 - y, j) for j in range(at.nx)], [[[]] * at.nx])
            self.got_y = at.along_y(send)
            return [self.got_y]
        if stage == 2:
            places, plan = [], []
            for j in offsets:
                places += [(0, j), (1, j), (2 + y, j)]
                plan.append([[], [], [(0, j)]])
            sends = self.add(gate, places, plan, [self.got_y])
            self.got_x = [at.along_x(send, j) for send, j in zip(sends, offsets)]
            return self.got_x
        if stage == 3:
            count = len(self.got_x)
            near, far = self.add(
                gate,
                [(1, 0), (2 + y, 0)],
                [[[(1 + n, 1) for n in range(count)]], [[(0, 0)] + [(1 + n, 2) for n in range(count)]]],
                [self.got_y] + self.got_x,
            )
            self.near = at.near_z(near)
            self.far = at.far_z(far)
            return [self.near, self.far]
        if stage == 4:
            terms = [self.near, self.far] + self.got_x
            (self.mine,) = self.add(gate, [(0, 0)], [[[(n, 0) for n in range(len(terms))]]], terms)
            self.last = at.along_y(self.mine)
            return [self.last]
        return []

    def total(self):
        return over_copies(self.at, self.mine.astype(jnp.float32) + self.last.astype(jnp.float32), 2)


def over_copies(at, total, bit):
    while bit < at.reps:
        total = total + at.flat(total.astype(jnp.bfloat16), bit * at.shards).astype(jnp.float32)
        bit *= 2
    return total


class Sum:
    def __init__(self, at, value):
        self.at = at
        self.value = value
        self.bit = 1

    def step(self, gate):
        if self.bit >= self.at.reps * self.at.shards:
            return []
        value = after(self.value, gate)
        self.value = value + self.at.flat(value, self.bit)
        self.bit *= 2
        return [self.value]

    def total(self):
        while self.step([]):
            pass
        return self.value


LOG2E = 1.4426950408889634
HEAD = 64
PAIR = 128
ROWS_Q = 256
ROWS_K = 256


def lanes_of(shape):
    return lax.broadcasted_iota(jnp.int32, shape, len(shape) - 1)


def half_turn(value):
    low = lanes_of(value.shape) % HEAD < HEAD // 2
    return jnp.where(low, pltpu.roll(value, PAIR - HEAD // 2, 1), pltpu.roll(value, HEAD // 2, 1))


def swap_matrix():
    left = lax.broadcasted_iota(jnp.int32, (PAIR, PAIR), 0)
    right = lax.broadcasted_iota(jnp.int32, (PAIR, PAIR), 1)
    return (left == (right ^ (HEAD // 2))).astype(jnp.bfloat16)


def two_parts(value):
    high = value.astype(jnp.bfloat16)
    return high, (value - high.astype(jnp.float32)).astype(jnp.bfloat16)


def head_sum(value):
    left = lax.broadcasted_iota(jnp.int32, (2 * PAIR, PAIR), 0) // HEAD % 2
    right = lax.broadcasted_iota(jnp.int32, (2 * PAIR, PAIR), 1) // HEAD
    same = (left == right).astype(jnp.bfloat16)
    parts = jnp.concatenate(two_parts(value), axis=1)
    return jnp.dot(parts, same, preferred_element_type=jnp.float32)


def turned(raw, cosine, sine):
    swapped = jnp.dot(raw, swap_matrix(), preferred_element_type=jnp.float32)
    rot = raw.astype(jnp.float32) * cosine + swapped * sine
    factor = lax.rsqrt(head_sum(rot * rot) + EPS)
    return rot * factor, factor


def only(value, head):
    mine = lanes_of(value.shape) // HEAD == head
    return jnp.where(mine, value, jnp.zeros_like(value))


def dot_last(a, b):
    return lax.dot_general(a, b, (((1,), (1,)), ((), ())), preferred_element_type=jnp.float32)


def dot_first(a, b):
    return lax.dot_general(a, b, (((0,), (0,)), ((), ())), preferred_element_type=jnp.float32)


FAR = -16384.0


def spare_lane(shape, head):
    return lanes_of(shape) - (1 - head) * HEAD


def query_lanes(value, head, segs):
    spare = spare_lane(value.shape, head)
    own = lanes_of(value.shape) // HEAD == head
    marks = (spare >= 0) & (spare < 8) & (spare != segs)
    return jnp.where(own, value.astype(jnp.float32), jnp.where(marks, FAR, 0.0)).astype(value.dtype)


def key_lanes(value, head, segs):
    spare = spare_lane(value.shape, head)
    own = lanes_of(value.shape) // HEAD == head
    return jnp.where(own, value.astype(jnp.float32), (spare == segs).astype(jnp.float32)).astype(value.dtype)


def attend_kernel(temper, q_ref, k_ref, v_ref, cos_ref, sin_ref, scale_ref, seg_ref, out_ref, lse_ref,
                  q_sc, k_sc, v_sc, sum_sc):
    length = q_ref.shape[0]
    bf16 = jnp.bfloat16
    f32 = jnp.float32
    scale = scale_ref[...]
    cosine = cos_ref[...]
    sine = sin_ref[...]
    segs = seg_ref[...]
    q2 = (turned(q_ref[...], cosine, sine)[0] * scale).astype(bf16)
    k2 = (turned(k_ref[...], cosine, sine)[0] * scale).astype(bf16)
    v = v_ref[...]
    ones = jnp.ones_like(v)
    for head in range(2):
        q_sc[head] = query_lanes(q2, head, segs)
        k_sc[head] = key_lanes(k2, head, segs)
        v_sc[head, :, :PAIR] = only(v, head)
        v_sc[head, :, PAIR:] = only(ones, head)
    factor = temper * LOG2E
    size = min(ROWS_Q, length)
    blocks = length // size
    causal = lax.broadcasted_iota(jnp.int32, (size, size), 0) >= lax.broadcasted_iota(
        jnp.int32, (size, size), 1
    )
    for block in range(blocks):
        at = block * size
        for head in range(2):
            keys = k_sc[head, at : at + size, :]
            raw = dot_last(q_sc[head, at:, :], keys)
            expo = causal_top(jnp.exp2(raw * factor), causal).astype(bf16)
            part = jnp.dot(expo, v_sc[head, at : at + size, :], preferred_element_type=f32)
            if block == 0 and head == 0:
                sum_sc[...] = part
            else:
                sum_sc[at:, :] += part
    mass = sum_sc[:, PAIR:]
    out_ref[...] = (sum_sc[:, :PAIR] / mass).astype(bf16)
    lse_ref[...] = jnp.log2(mass)


def causal_top(value, causal):
    size = causal.shape[0]
    edge = jnp.where(causal, value[:size, :], 0.0)
    if value.shape[0] == size:
        return edge
    return jnp.concatenate([edge, value[size:, :]], axis=0)


def causal_bottom(value, causal):
    size = causal.shape[0]
    edge = jnp.where(causal, value[-size:, :], 0.0)
    if value.shape[0] == size:
        return edge
    return jnp.concatenate([value[:-size, :], edge], axis=0)


def pair_spec(length, offset):
    return pl.BlockSpec((length, PAIR), lambda p: (0, p + offset))


def attention(qkv, cosine, sine, scale, segs, offset):
    length, width = qkv.shape[0], qkv.shape[1] // 3
    pairs = width // PAIR
    whole = pl.BlockSpec((length, PAIR), lambda p: (0, 0))
    column = pl.BlockSpec((length, 1), lambda p: (0, 0))
    return pl.pallas_call(
        partial(attend_kernel, math.sqrt(HEAD)),
        grid=(pairs,),
        in_specs=[
            pair_spec(length, 0), pair_spec(length, pairs), pair_spec(length, 2 * pairs),
            whole, whole, pl.BlockSpec((1, PAIR), lambda p: (0, p + offset // PAIR)), column,
        ],
        out_specs=[pair_spec(length, 0), pair_spec(length, 0)],
        scratch_shapes=[
            pltpu.VMEM((2, length, PAIR), jnp.bfloat16),
            pltpu.VMEM((2, length, PAIR), jnp.bfloat16),
            pltpu.VMEM((2, length, 2 * PAIR), jnp.bfloat16),
            pltpu.VMEM((length, 2 * PAIR), jnp.float32),
        ],
        out_shape=[
            far_array((length, width), jnp.bfloat16),
            far_array((length, width), jnp.float32),
        ],
        compiler_params=pltpu.CompilerParams(vmem_limit_bytes=40 << 20),
        cost_estimate=pl.CostEstimate(
            flops=16 * length * length * width // 2, bytes_accessed=8 * length * width,
            transcendentals=length * length * width // HEAD // 2,
        ),
        name="attend",
    )(qkv, qkv, qkv, cosine, sine, scale, segs)


def three_parts(value):
    high = value.astype(jnp.bfloat16).astype(jnp.float32)
    rest = value - high
    mid = rest.astype(jnp.bfloat16).astype(jnp.float32)
    return high, mid, rest - mid


def attend_back_kernel(temper, q_ref, k_ref, v_ref, o_ref, g_ref, cos_ref, sin_ref, scale_ref, seg_ref, lse_ref,
                       g3_ref, gs_ref, q_sc, k_sc, v_sc, g_sc, qo_sc, go_sc, dq_sc, dk_sc, dv_sc):
    length = q_ref.shape[0]
    bf16 = jnp.bfloat16
    f32 = jnp.float32
    scale = scale_ref[...]
    cosine = cos_ref[...]
    sine = sin_ref[...]
    segs = seg_ref[...]
    qn, q_factor = turned(q_ref[...], cosine, sine)
    kn, k_factor = turned(k_ref[...], cosine, sine)
    q2 = (qn * scale).astype(bf16)
    k2 = (kn * scale).astype(bf16)
    v = v_ref[...]
    grad = g_ref[...]
    spread = head_sum(grad.astype(f32) * o_ref[...].astype(f32))
    factor = temper * LOG2E
    lanes = lanes_of((length, PAIR))
    for head in range(2):
        spare = spare_lane((length, PAIR), head)
        own = lanes // HEAD == head
        parts = three_parts(lse_ref[:, head * HEAD : head * HEAD + 1] * (-1.0 / factor))
        marks = jnp.where((spare >= 0) & (spare < 8) & (spare != segs), FAR, 0.0)
        for n in range(3):
            marks = jnp.where(spare == 8 + n, parts[n], marks)
        q_sc[head] = jnp.where(own, q2.astype(f32), marks).astype(bf16)
        k_sc[head] = jnp.where(
            own, k2.astype(f32), ((spare == segs) | ((spare >= 8) & (spare < 11))).astype(f32)
        ).astype(bf16)
        parts = three_parts(-spread[:, head * HEAD : head * HEAD + 1])
        marks = jnp.zeros((length, PAIR), f32)
        for n in range(3):
            marks = jnp.where(spare == n, parts[n], marks)
        g_sc[head] = jnp.where(own, grad.astype(f32), marks).astype(bf16)
        v_sc[head] = jnp.where(own, v.astype(f32), ((spare >= 0) & (spare < 3)).astype(f32)).astype(bf16)
        qo_sc[head] = only(q2, head)
        go_sc[head] = only(grad, head)
    size = min(ROWS_K, length)
    causal = lax.broadcasted_iota(jnp.int32, (size, size), 0) <= lax.broadcasted_iota(
        jnp.int32, (size, size), 1
    )
    blocks = length // size
    lanes = lanes_of((size, PAIR)) // HEAD
    for block in range(blocks - 1, -1, -1):
        at = block * size
        end = at + size
        dqs = []
        for head in range(2):
            keys = k_sc[head, :end, :]
            probs = causal_bottom(jnp.exp2(dot_last(keys, q_sc[head, at:end, :]) * factor), causal)
            ds = (probs * dot_last(v_sc[head, :end, :], g_sc[head, at:end, :])).astype(bf16)
            dv = jnp.dot(probs.astype(bf16), go_sc[head, at:end, :], preferred_element_type=f32)
            dk = jnp.dot(ds, qo_sc[head, at:end, :], preferred_element_type=f32)
            dqs.append(dot_first(ds, keys))
            if block == blocks - 1 and head == 0:
                dv_sc[...] = dv
                dk_sc[...] = dk
            else:
                dv_sc[:end, :] += dv
                dk_sc[:end, :] += dk
        dq_sc[at:end, :] = jnp.where(lanes == 0, dqs[0], dqs[1])
    g3_ref[2] = dv_sc[...].astype(bf16)
    dq = dq_sc[...] * temper
    dk = dk_sc[...] * temper
    gs_ref[0] = jnp.broadcast_to(jnp.sum(dq * qn + dk * kn, axis=0, keepdims=True), (8, PAIR))

    def unturn(grad, unit, unit_factor):
        grad = grad * scale
        rot = unit_factor * (grad - unit * head_sum(grad * unit))
        return (rot * cosine + half_turn(rot * sine)).astype(bf16)

    g3_ref[0] = unturn(dq, qn, q_factor)
    g3_ref[1] = unturn(dk, kn, k_factor)


def attention_back(qkv, out, grad, lse, cosine, sine, scale, segs, offset, first, pairs):
    length, width = qkv.shape[0], qkv.shape[1] // 3
    every = width // PAIR
    base = offset // PAIR
    whole = pl.BlockSpec((length, PAIR), lambda p: (0, 0))
    column = pl.BlockSpec((length, 1), lambda p: (0, 0))
    return pl.pallas_call(
        partial(attend_back_kernel, math.sqrt(HEAD)),
        grid=(pairs,),
        in_specs=[
            pair_spec(length, first), pair_spec(length, first + every), pair_spec(length, first + 2 * every),
            pair_spec(length, first), pair_spec(length, first + base),
            whole, whole, pl.BlockSpec((1, PAIR), lambda p: (0, p + first + base)), column, pair_spec(length, first),
        ],
        out_specs=[
            pl.BlockSpec((3, length, PAIR), lambda p: (0, 0, p)),
            pl.BlockSpec((1, 8, PAIR), lambda p: (p, 0, 0)),
        ],
        scratch_shapes=[pltpu.VMEM((2, length, PAIR), jnp.bfloat16)] * 6
        + [pltpu.VMEM((length, PAIR), jnp.float32)] * 3,
        out_shape=[
            far_array((3, length, pairs * PAIR), jnp.bfloat16),
            jax.ShapeDtypeStruct((pairs, 8, PAIR), jnp.float32),
        ],
        compiler_params=pltpu.CompilerParams(vmem_limit_bytes=48 << 20),
        cost_estimate=pl.CostEstimate(
            flops=60 * length * length * pairs * PAIR, bytes_accessed=18 * length * pairs * PAIR,
            transcendentals=length * length * pairs * 2,
        ),
        name="attend_back",
    )(far(qkv), far(qkv), far(qkv), far(out), far(grad), far(cosine), far(sine), scale, far(segs), far(lse))


def rotary_wide(positions):
    half = HEAD // 2
    freq = jnp.power(10000.0, -2.0 * jnp.arange(half, dtype=jnp.float32) / HEAD)
    angle = positions.astype(jnp.float32)[:, None] * freq
    cosine = jnp.cos(angle)
    sine = jnp.sin(angle)
    return (
        jnp.concatenate([cosine] * 4, axis=1),
        jnp.concatenate([-sine, sine, -sine, sine], axis=1),
    )


def far_array(shape, kind):
    return pltpu.HBM(shape, kind)


def far(value):
    return pltpu.with_memory_space_constraint(value, pltpu.HBM)


def mean_last(value):
    return jnp.mean(value, axis=-1, keepdims=True)


def sort_matrix(core, each):
    left = lax.broadcasted_iota(jnp.int32, (256, 256), 0)
    right = lax.broadcasted_iota(jnp.int32, (256, 256), 1)
    place = right % 128
    source = (place // each * 2 + (core + 1 + right // 128) % 2) * each + place % each
    return (left == source).astype(jnp.bfloat16)


def sort_cores(value, matrix, out_ref, start):
    half = out_ref.shape[1] // 2
    for n in range(value.shape[1] // 256):
        both = jnp.dot(value[:, 256 * n : 256 * (n + 1)], matrix, preferred_element_type=jnp.float32)
        at = start + 128 * n
        out_ref[:, at : at + 128] = both[:, :128].astype(jnp.bfloat16)
        out_ref[:, half + at : half + at + 128] = both[:, 128:].astype(jnp.bfloat16)


def sort_kernel(each, core_ref, value_ref, out_ref):
    sort_cores(value_ref[...], sort_matrix(core_ref[0], each), out_ref, 0)


def sorted_cores(value, core, each):
    rows, width = value.shape
    tile = min(512, rows)
    spec = pl.BlockSpec((tile, width), lambda i: (i, 0))
    return pl.pallas_call(
        partial(sort_kernel, each),
        grid=(rows // tile,),
        in_specs=[pl.BlockSpec(memory_space=pltpu.SMEM), spec],
        out_specs=spec,
        out_shape=jax.ShapeDtypeStruct((rows, width), value.dtype),
        cost_estimate=pl.CostEstimate(flops=512 * rows * width, bytes_accessed=4 * rows * width, transcendentals=0),
        name="sort_cores",
    )(core, value)


def after_attention_kernel(each, core_ref, a0_ref, a1_ref, w_ref, x_ref, alpha_ref,
                           branch_ref, h_ref, low_ref, hs_ref):
    f32 = jnp.float32
    half = a0_ref.shape[1]
    matrix = sort_matrix(core_ref[0], each)
    branch = jnp.dot(a0_ref[...], w_ref[:half, :], preferred_element_type=f32)
    branch = branch + jnp.dot(a1_ref[...], w_ref[half:, :], preferred_element_type=f32)
    branch_ref[...] = branch
    unit = branch * lax.rsqrt(mean_last(branch * branch) + EPS)
    x = x_ref[...].astype(f32)
    z = x + alpha_ref[...] * (unit - x)
    h = z * lax.rsqrt(mean_last(z * z) + EPS)
    low = h.astype(jnp.bfloat16)
    h_ref[...] = h
    low_ref[...] = low
    sort_cores(low, matrix, hs_ref, 0)


def after_attention(core, each, att, w_out, tokens, alpha):
    rows, width = tokens.shape
    tile = min(512, rows)
    full = pl.BlockSpec((tile, width), lambda i: (i, 0))
    half = pl.BlockSpec((tile, width // 2), lambda i: (i, 0))
    shape = lambda cols, kind: jax.ShapeDtypeStruct((rows, cols), kind)
    return pl.pallas_call(
        partial(after_attention_kernel, each),
        grid=(rows // tile,),
        in_specs=[
            pl.BlockSpec(memory_space=pltpu.SMEM), half, half,
            pl.BlockSpec((width, width), lambda i: (0, 0)), full, pl.BlockSpec((1, width), lambda i: (0, 0)),
        ],
        out_specs=[full] * 4,
        out_shape=[
            far_array((rows, width), jnp.float32), far_array((rows, width), jnp.float32),
            shape(width, jnp.bfloat16), far_array((rows, width), jnp.bfloat16),
        ],
        compiler_params=pltpu.CompilerParams(vmem_limit_bytes=40 << 20),
        cost_estimate=pl.CostEstimate(flops=2 * rows * width * width, bytes_accessed=20 * rows * width, transcendentals=0),
        name="after_attention",
    )(core, *att, w_out, tokens, alpha)


def sigmoid(value):
    return 0.5 * jnp.tanh(0.5 * value) + 0.5


def up_kernel(h_ref, wu_ref, wg_ref, su_ref, sg_ref, *refs):
    f32 = jnp.float32
    bf16 = jnp.bfloat16
    up_ref, gate_ref, hid_ref = refs[-3:]
    up = jnp.dot(h_ref[...], wu_ref[...], preferred_element_type=f32)
    gate = jnp.dot(h_ref[...], wg_ref[...], preferred_element_type=f32)
    value = gate * sg_ref[...]
    up_ref[...] = up.astype(bf16)
    gate_ref[...] = gate.astype(bf16)
    hid_ref[...] = (up * su_ref[...] * (value * sigmoid(value))).astype(bf16)


def feed_up(part, parts, h_low, w, scale_up, scale_gate, before):
    rows, width = h_low.shape
    ff = scale_up.shape[1]
    q = w.shape[1] // 2
    block = min(512, q)
    steps = q // block
    first = part * steps
    out = pl.BlockSpec((rows, block), lambda j: (0, first + j))
    line = pl.BlockSpec((1, block), lambda j: (0, first + j))
    shape = far_array((rows, ff), jnp.bfloat16)
    return pl.pallas_call(
        up_kernel,
        grid=(steps,),
        in_specs=[
            pl.BlockSpec((rows, width), lambda j: (0, 0)),
            pl.BlockSpec((width, block), lambda j: (0, j)),
            pl.BlockSpec((width, block), lambda j: (0, steps + j)),
            line, line,
        ] + [pl.BlockSpec(memory_space=pl.ANY)] * len(before),
        out_specs=[out] * 3,
        out_shape=[shape] * 3,
        input_output_aliases={5 + n: n for n in range(len(before))},
        compiler_params=pltpu.CompilerParams(vmem_limit_bytes=48 << 20),
        cost_estimate=pl.CostEstimate(flops=4 * rows * width * q, bytes_accessed=2 * (rows * width + 2 * width * q + 3 * rows * q), transcendentals=rows * q),
        name="feed_up",
    )(h_low, w, w, scale_up, scale_gate, *before)


def finish_kernel(steps, hid_ref, w0_ref, w1_ref, h1_ref, t_ref, mask_ref, alpha_ref,
                  out_ref, gm_ref, gz_ref, ga_ref, loss_ref, acc):
    f32 = jnp.float32
    bf16 = jnp.bfloat16
    step = pl.program_id(0)
    half = w0_ref.shape[1]

    @pl.when(step == 0)
    def _():
        acc[...] = jnp.zeros_like(acc)

    acc[:, :half] += jnp.dot(hid_ref[...], w0_ref[...], preferred_element_type=f32)
    acc[:, half:] += jnp.dot(hid_ref[...], w1_ref[...], preferred_element_type=f32)

    @pl.when(step == steps - 1)
    def _():
        alpha = alpha_ref[...]
        grads = jnp.zeros(ga_ref.shape, f32)
        losses = jnp.zeros(loss_ref.shape, f32)
        tile = min(256, acc.shape[0])
        for at in range(0, acc.shape[0], tile):
            rows = pl.ds(at, tile)
            branch = acc[rows, :]
            factor = lax.rsqrt(mean_last(branch * branch) + EPS)
            unit = branch * factor
            h1 = h1_ref[rows, :]
            z = h1 + alpha * (unit - h1)
            z_factor = lax.rsqrt(mean_last(z * z) + EPS)
            h2 = z * z_factor
            out_ref[rows, :] = h2.astype(bf16)
            diff = h2 - t_ref[rows, :].astype(f32)
            masked = mask_ref[rows, :] * diff
            grad = 2.0 * masked
            gz = z_factor * (grad - h2 * mean_last(grad * h2))
            gz_ref[rows, :] = (1.0 - alpha) * gz
            back = alpha * gz
            gm_ref[rows, :] = (factor * (back - unit * mean_last(back * unit))).astype(bf16)
            grads = grads + jnp.sum(gz * (unit - h1), axis=0, keepdims=True)
            losses = losses + jnp.sum(masked * diff, axis=0, keepdims=True)
        ga_ref[...] = grads
        loss_ref[...] = losses


def finish(hidden, down, h1, teacher, mask, alpha):
    rows, ff = hidden.shape
    width = h1.shape[1]
    block = min(1024, ff)
    steps = ff // block
    once = pl.Buffered(1)
    whole = lambda cols=width: pl.BlockSpec((rows, cols), lambda j: (0, 0), pipeline_mode=once)
    row = pl.BlockSpec((1, width), lambda j: (0, 0))
    deep = pl.BlockSpec((block, width // 2), lambda j: (j, 0))
    line = jax.ShapeDtypeStruct((1, width), jnp.float32)
    return pl.pallas_call(
        partial(finish_kernel, steps),
        grid=(steps,),
        in_specs=[
            pl.BlockSpec((rows, block), lambda j: (0, j)),
            deep, deep, whole(), whole(), whole(1), row,
        ],
        out_specs=[whole(), whole(), whole(), row, row],
        out_shape=[
            far_array((rows, width), jnp.bfloat16), jax.ShapeDtypeStruct((rows, width), jnp.bfloat16),
            far_array((rows, width), jnp.float32), line, line,
        ],
        scratch_shapes=[pltpu.VMEM((rows, width), jnp.float32)],
        compiler_params=pltpu.CompilerParams(vmem_limit_bytes=48 << 20),
        cost_estimate=pl.CostEstimate(flops=2 * rows * width * ff, bytes_accessed=2 * (rows + width) * ff + 16 * rows * width, transcendentals=0),
        name="finish",
    )(hidden, *down, h1, teacher, mask, alpha)


def feed_back_kernel(steps, each, last, g_ref, left_ref, w0_ref, w1_ref, up_ref, gate_ref, su_ref, sg_ref, wu_ref, wg_ref, start_ref, *refs):
    f32 = jnp.float32
    bf16 = jnp.bfloat16
    step = pl.program_id(0)
    half = w0_ref.shape[1]
    if last:
        branch_ref, x_ref, alpha_ref, gsu_ref, gsg_ref, other_ref, own_ref, gb_ref, gx_ref, ga_ref, acc = refs
        parts = (other_ref, own_ref)
    else:
        gsu_ref, gsg_ref, all_ref, acc = refs
        parts = (all_ref,)

    @pl.when(step == 0)
    def _():
        acc[...] = start_ref[...]

    su = su_ref[...]
    sg = sg_ref[...]
    back = dot_last(g_ref[:, :half], w0_ref[...]) + dot_last(g_ref[:, half:], w1_ref[...])
    up = up_ref[...].astype(f32)
    gate = gate_ref[...].astype(f32)
    value = gate * sg
    sig = sigmoid(value)
    active = value * sig
    with_active = back * active
    g_value = back * up * su * (sig + active * (1.0 - sig))
    g_up = (with_active * su).astype(bf16)
    g_gate = (g_value * sg).astype(bf16)
    gsu_ref[...] = jnp.sum(with_active * up, axis=0, keepdims=True)
    gsg_ref[...] = jnp.sum(g_value * gate, axis=0, keepdims=True)
    acc[...] += dot_last(g_up, wu_ref[...])
    acc[...] += dot_last(g_gate, wg_ref[...])
    for n, grad in enumerate((g_up, g_gate)):
        rows = dot_first(left_ref[...], grad).astype(bf16)
        at = 0
        for part in parts:
            for group in range(part.shape[0]):
                part[group, n] = rows[at : at + each, :]
                at += each
    if not last:
        return

    @pl.when(step == steps - 1)
    def _():
        alpha = alpha_ref[...]
        tile = min(256, acc.shape[0])
        total = jnp.zeros(ga_ref.shape, f32)
        for at in range(0, acc.shape[0], tile):
            branch = branch_ref[at : at + tile, :]
            a_factor = lax.rsqrt(mean_last(branch * branch) + EPS)
            unit = branch * a_factor
            x = x_ref[at : at + tile, :].astype(f32)
            z = x + alpha * (unit - x)
            z_factor = lax.rsqrt(mean_last(z * z) + EPS)
            h = z * z_factor
            grad = acc[at : at + tile, :]
            gz = z_factor * (grad - h * mean_last(grad * h))
            total = total + jnp.sum(gz * (unit - x), axis=0, keepdims=True)
            back = alpha * gz
            gb_ref[at : at + tile, :] = (a_factor * (back - unit * mean_last(back * unit))).astype(bf16)
            gx_ref[at : at + tile, :] = (1.0 - alpha) * gz
        ga_ref[...] = total


def feed_back(part, parts, shards, g, left, down, up, gate, scale_up, scale_gate, w, start, rest=None):
    rows, width = g.shape
    ff = up.shape[1]
    block = min(512, ff // parts)
    steps = ff // parts // block
    first = part * steps
    each = width // shards
    last = rest is not None
    once = pl.Buffered(1)
    whole = lambda: pl.BlockSpec((rows, width), lambda j: (0, 0), pipeline_mode=once)
    col = pl.BlockSpec((rows, block), lambda j: (0, first + j))
    line = pl.BlockSpec((1, block), lambda j: (0, first + j))
    sums = pl.BlockSpec((1, block), lambda j: (0, j))
    row = pl.BlockSpec((1, width), lambda j: (0, 0))
    deep = pl.BlockSpec((block, width // 2), lambda j: (first + j, 0))
    small = jax.ShapeDtypeStruct((1, ff // parts), jnp.float32)
    specs = [
        whole(), whole(), deep, deep, col, col, line, line,
        pl.BlockSpec((width, block), lambda j: (0, j)),
        pl.BlockSpec((width, block), lambda j: (0, steps + j)),
        whole(),
    ]
    operands = [g, left, *down, up, gate, scale_up, scale_gate, w, w, start]
    groups = shards // 2 if last else shards
    grads = pl.BlockSpec((groups, 2, each, block), lambda j: (0, 0, 0, j))
    shape = far_array((groups, 2, each, ff // parts), jnp.bfloat16)
    full = jax.ShapeDtypeStruct((rows, width), jnp.float32)
    scratch = []
    if last:
        specs += [whole(), whole(), row]
        operands += rest
        out_specs = [sums, sums, grads, grads, whole(), whole(), row]
        out_shape = [small, small, shape, shape, jax.ShapeDtypeStruct((rows, width), jnp.bfloat16), far_array((rows, width), jnp.float32),
                     jax.ShapeDtypeStruct((1, width), jnp.float32)]
        scratch = [pltpu.VMEM((rows, width), jnp.float32)]
    else:
        out_specs = [sums, sums, grads, pl.BlockSpec((rows, width), lambda j: (0, 0), pipeline_mode=once)]
        out_shape = [small, small, shape, full]
    return pl.pallas_call(
        partial(feed_back_kernel, steps, each, last),
        grid=(steps,),
        in_specs=specs,
        out_specs=out_specs,
        out_shape=out_shape,
        scratch_shapes=scratch,
        compiler_params=pltpu.CompilerParams(vmem_limit_bytes=61 << 20),
        cost_estimate=pl.CostEstimate(flops=10 * rows * width * ff // parts, bytes_accessed=10 * (rows + width) * ff // parts + 16 * rows * width, transcendentals=rows * ff // parts),
        name="feed_back",
    )(*operands)


def down_grad_kernel(each, core_ref, h_ref, g_ref, other_ref, own_ref, whole_ref):
    whole_ref[...] = dot_first(h_ref[...], g_ref[...])
    core = core_ref[0]
    for n in range(h_ref.shape[1] // (2 * each)):
        for out_ref, which in ((other_ref, 1 - core), (own_ref, core)):
            start = pl.multiple_of((2 * n + which) * each, each)
            out_ref[n * each : (n + 1) * each, :] = whole_ref[pl.ds(start, each), :].astype(jnp.bfloat16)


def down_grad(core, hidden, g, groups):
    rows, ff = hidden.shape
    width = g.shape[1]
    each = ff // (2 * groups)
    block = min(1024, ff)
    out = pl.BlockSpec((block // 2, width), lambda i: (i, 0))
    shape = far_array((ff // 2, width), jnp.bfloat16)
    return pl.pallas_call(
        partial(down_grad_kernel, each),
        grid=(ff // block,),
        in_specs=[
            pl.BlockSpec(memory_space=pltpu.SMEM),
            pl.BlockSpec((rows, block), lambda i: (0, i)),
            pl.BlockSpec((rows, width), lambda i: (0, 0)),
        ],
        out_specs=[out, out],
        out_shape=[shape, shape],
        scratch_shapes=[pltpu.VMEM((block, width), jnp.float32)],
        compiler_params=pltpu.CompilerParams(vmem_limit_bytes=40 << 20),
        cost_estimate=pl.CostEstimate(flops=2 * rows * ff * width, bytes_accessed=2 * rows * ff + 2 * ff * width + 2 * rows * width, transcendentals=0),
        name="down_grad",
    )(core, hidden, g)


def row_grad_kernel(left_ref, *refs):
    rights, (other_ref, own_ref) = refs[:-2], refs[-2:]
    half = other_ref.shape[0]
    at = 0
    for right in rights:
        cols = right.shape[1]
        both = dot_first(left_ref[...], right[...])
        other_ref[:, at : at + cols] = both[:half, :].astype(jnp.bfloat16)
        own_ref[:, at : at + cols] = both[half:, :].astype(jnp.bfloat16)
        at += cols


def rows_kernel(count, *refs):
    lefts, rights, out_ref = refs[:count], refs[count:-1], refs[-1]
    at = 0
    for left in lefts:
        row = left.shape[1]
        col = 0
        for right in rights:
            cols = right.shape[1]
            out_ref[at : at + row, col : col + cols] = dot_first(left[...], right[...]).astype(jnp.bfloat16)
            col += cols
        at += row


def out_grad(lefts, right, total):
    rows, width = right.shape
    every = sum(left.shape[1] for left in lefts)
    block = min(512, width)
    return pl.pallas_call(
        partial(rows_kernel, len(lefts)),
        grid=(width // block,),
        in_specs=[pl.BlockSpec(left.shape, lambda j: (0, 0)) for left in lefts]
        + [pl.BlockSpec((rows, block), lambda j: (0, j))],
        out_specs=pl.BlockSpec((every, block), lambda j: (0, j)),
        out_shape=far_array((every, total), jnp.bfloat16),
        compiler_params=pltpu.CompilerParams(vmem_limit_bytes=40 << 20),
        cost_estimate=pl.CostEstimate(flops=2 * rows * width * every, bytes_accessed=2 * (rows * (width + every) + width * every), transcendentals=0),
        name="out_grad",
    )(*lefts, right)


def heads_grad(left, parts, before=None, wide=0):
    rows, width = left.shape
    cols = parts[0].shape[2]
    count = len(parts)
    each = cols * count
    lefts = pl.BlockSpec((rows, width), lambda j: (0, 0))
    rights = [pl.BlockSpec((pl.Squeezed(), rows, cols), lambda j: (j, 0, 0))] * count
    params = dict(
        compiler_params=pltpu.CompilerParams(vmem_limit_bytes=40 << 20),
        cost_estimate=pl.CostEstimate(flops=6 * rows * width * each, bytes_accessed=2 * (rows * width + 3 * (width + rows) * each), transcendentals=0),
        name="heads_grad",
    )
    if before is None:
        out = pl.BlockSpec((width // 2, each), lambda j: (0, j))
        shape = far_array((width // 2, 3 * each + wide), jnp.bfloat16)
        return pl.pallas_call(
            row_grad_kernel, grid=(3,), in_specs=[lefts] + rights, out_specs=[out, out], out_shape=[shape, shape], **params
        )(left, *parts)
    first = before.shape[1] // each - 3
    return pl.pallas_call(
        rows_under_kernel,
        grid=(3,),
        in_specs=[lefts] + rights + [pl.BlockSpec(memory_space=pl.ANY)],
        out_specs=pl.BlockSpec((width, each), lambda j: (0, first + j)),
        out_shape=far_array(before.shape, jnp.bfloat16),
        input_output_aliases={1 + count: 0},
        **params,
    )(left, *parts, before)


def rows_under_kernel(left_ref, *refs):
    rows_kernel(1, left_ref, *refs[:-2], refs[-1])


def input_grad_kernel(scale_ref, base_ref, *refs):
    out_ref = refs[-1]
    total = base_ref[...]
    for n in range(len(refs) // 2):
        part, w = refs[2 * n : 2 * n + 2]
        cols = part.shape[2]
        for p in range(3):
            total = total + dot_last(part[p], w[:, p * cols : (p + 1) * cols])
    out_ref[...] = total * scale_ref[0]


def input_grad(scale, base, parts, weights):
    rows, width = base.shape
    tile = min(256, width)
    out = pl.BlockSpec((rows, tile), lambda j: (0, j))
    specs, operands = [], []
    for part, w in zip(parts, weights):
        specs.append(pl.BlockSpec(part.shape, lambda j: (0, 0, 0), pipeline_mode=pl.Buffered(1)))
        specs.append(pl.BlockSpec((tile, w.shape[1]), lambda j: (j, 0)))
        operands += [part, w]
    flops = 2 * rows * width * sum(w.shape[1] for w in weights)
    return pl.pallas_call(
        input_grad_kernel,
        grid=(width // tile,),
        in_specs=[pl.BlockSpec(memory_space=pltpu.SMEM), out] + specs,
        out_specs=out,
        out_shape=jax.ShapeDtypeStruct((rows, width), jnp.float32),
        compiler_params=pltpu.CompilerParams(vmem_limit_bytes=48 << 20),
        cost_estimate=pl.CostEstimate(flops=flops, bytes_accessed=20 * rows * width, transcendentals=0),
        name="input_grad",
    )(scale, base, *operands)


def slots_kernel(plan, rows, extras, slots, keep, got, *refs):
    f32 = jnp.float32
    terms = refs[:extras]
    outs = refs[extras : extras + len(plan)]
    kept, gotten, sems = refs[extras + len(plan) :]
    total = sum(len(blocks) for blocks in plan)
    copies = []
    for b in range(total):
        place = pl.ds(pl.multiple_of(slots[b] * rows, rows), rows)
        pair = (
            pltpu.make_async_copy(keep.at[place], kept.at[b], sems.at[0, b]),
            pltpu.make_async_copy(got.at[place], gotten.at[b], sems.at[1, b]),
        )
        for copy in pair:
            copy.start()
        copies.append(pair)
    b = 0
    for out, blocks in zip(outs, plan):
        for n, uses in enumerate(blocks):
            for copy in copies[b]:
                copy.wait()
            value = kept[b].astype(f32) + gotten[b].astype(f32)
            for term, at in uses:
                value = value + terms[term][at * rows : (at + 1) * rows, :].astype(f32)
            out[n * rows : (n + 1) * rows, :] = value.astype(out.dtype)
            b += 1


def add_slots(keep, got, rows, slots, plan, terms=()):
    cols = keep.shape[1]
    total = len(slots)
    vmem = pl.BlockSpec(memory_space=pltpu.VMEM)
    block = rows * cols
    return pl.pallas_call(
        partial(slots_kernel, plan, rows, len(terms)),
        in_specs=[pl.BlockSpec(memory_space=pltpu.SMEM)] + [pl.BlockSpec(memory_space=pl.ANY)] * 2 + [vmem] * len(terms),
        out_specs=[vmem] * len(plan),
        out_shape=[jax.ShapeDtypeStruct((len(blocks) * rows, cols), keep.dtype) for blocks in plan],
        scratch_shapes=[
            pltpu.VMEM((total, rows, cols), keep.dtype),
            pltpu.VMEM((total, rows, cols), keep.dtype),
            pltpu.SemaphoreType.DMA((2, total)),
        ],
        compiler_params=pltpu.CompilerParams(vmem_limit_bytes=8 * total * block + 8 * block + (4 << 20)),
        cost_estimate=pl.CostEstimate(flops=0, bytes_accessed=8 * total * block, transcendentals=0),
        name="add_slots",
    )(jnp.stack(slots).astype(jnp.int32), far(keep), far(got), *terms)


def body(
    tokens,
    teacher,
    valid,
    segments,
    positions,
    w_qkv,
    w_out,
    w_upgate,
    w_down,
    s_qk,
    alpha_attn,
    s_up,
    s_gate,
    alpha_mlp,
):
    f32 = jnp.float32
    bf16 = jnp.bfloat16
    at = Place()
    rows, width = tokens.shape
    ff = w_upgate.shape[1] // 2
    each = w_out.shape[0]
    groups = at.shards // NC
    core = at.core.reshape(1).astype(jnp.int32)
    half = width // 2
    pairs = half // PAIR
    segs = segments.reshape(rows, 1)

    def columns(w, starts, size):
        return jnp.concatenate([w[:, s : s + size] for s in starts], axis=1)

    chunks = [columns(w_qkv, [p * width + n * half for p in range(3)], half) for n in range(2)]
    vectors = (s_qk, alpha_attn, s_up, s_gate, alpha_mlp)
    short = jnp.concatenate(vectors).reshape(each, -1)
    per_row = short.shape[1]
    chunks[0] = jnp.concatenate([chunks[0], jnp.pad(short, ((0, 0), (0, PAIR - per_row)))], axis=1)
    chunks.append(w_out)
    chunks += [w_down[:, :half], w_down[:, half:]]

    gather = Gather(at, chunks[:3])
    late = Gather(at, chunks[3:])
    mask = valid.astype(f32)
    upgate = [
        lax.all_gather(columns(w_upgate, [n * ff // 2, ff + n * ff // 2], ff // 2), "shard", axis=0, tiled=True)
        for n in range(2)
    ]
    gate = []
    for tick in range(4):
        moved = gather.tick(tick, gate)
        if tick == 3:
            late.tick(0, gate)
        if tick == 0:
            cosine, sine = rotary_wide(positions.reshape(rows))
            moved += [cosine, sine]
        if tick == 1:
            x_sorted = sorted_cores(after(tokens, gate + gather.sends), core, each)
            moved += [x_sorted]
        gate = moved
    def dot(left, right):
        return jnp.dot(left, right, preferred_element_type=f32).astype(bf16)

    weights, qkv, att, lse = {}, [], [], []
    for n in range(2):
        moved = gather.tick(4 + n, gate)
        gate = gate + gather.sends
        weights[n] = gather.full(n)
        if n == 0:
            found = weights[0][:, 3 * half : 3 * half + per_row].astype(f32).reshape(at.shards, -1)
            shorts, place = [], 0
            for vector in vectors:
                size = vector.shape[0]
                shorts.append(found[:, place : place + size].reshape(1, -1))
                place += size
            f_sqk, f_aa, f_su, f_sg, f_am = shorts
        qkv.append(dot(after(tokens, gate), weights[n][:, : 3 * half]))
        late.tick(1 + n, [qkv[n]], True)
        out, sums = attention(qkv[n], cosine, sine, f_sqk, segs, n * half)
        att.append(out)
        lse.append(sums)
        gate = moved + [out]
    late.tick(3, gate)
    weights[2] = gather.full(2)
    att = [after(a, gate) for a in att]
    branch_a, h_one, h_low, h_sorted = after_attention(
        core, each, [far(a) for a in att], weights[2], tokens, f_aa
    )
    before = feed_up(0, 2, h_low, upgate[0], f_su, f_sg, [])
    late.tick(4, [before[2]])
    before = feed_up(1, 2, after(h_low, [before[2]]), upgate[1], f_su, f_sg, before)
    down = [late.full(0), late.full(1)]
    up, gate_part, hidden = before
    output, g_bm, gz, grad_am, loss_rows = finish(
        hidden, down, h_one, teacher, mask.reshape(rows, 1), f_am
    )

    waiting = {}

    def window(gate, names, late=()):
        moved = []
        sends = list(gate)
        for name in names:
            moved += waiting[name].step(gate)
            sends += waiting[name].sends
        for name in late:
            waiting[name].step(gate)
            sends += waiting[name].sends
        return moved, sends

    upper = lax.broadcasted_iota(jnp.int32, (8, 128), 0) < 4
    counted = Sum(at, jnp.where(upper, jnp.sum(loss_rows), jnp.sum(mask)))
    waiting["down"] = Reduce(at, *down_grad(core, hidden, g_bm, groups))
    gate = [waiting["down"].send, waiting["down"].keep]
    moved, gate = window(gate, ["down"])
    moved += counted.step(gate)
    su0, sg0, first_up, acc = feed_back(
        0, 2, at.shards, after(g_bm, gate), h_low, down, up, gate_part, f_su, f_sg, upgate[0], gz
    )
    gate = moved + [acc]
    moved, gate = window(gate, ["down"])
    moved += counted.step(gate)
    first_up = lax.psum_scatter(after(first_up, gate), "shard", scatter_dimension=0, tiled=True)
    su1, sg1, up_other, up_own, g_ba, gx_base, grad_aa = feed_back(
        1, 2, at.shards, after(g_bm, gate), h_sorted, down, up, gate_part, f_su, f_sg, upgate[1], acc,
        [branch_a, tokens, f_aa],
    )
    waiting["up"] = Reduce(at, up_other.reshape(width, ff // 2), up_own.reshape(width, ff // 2))
    gate = moved + [g_ba]

    g3, g_scale = {}, []

    def back(n, gate):
        out, sums = attention_back(
            qkv[n], att[n], after(g_att, gate), lse[n], cosine, sine, f_sqk, segs, n * half, 0, pairs
        )
        g3[n] = out
        g_scale.append(sums[:, 0, :].reshape(-1))
        return [out]

    moved, gate = window(gate, ["up"], ["down"])
    moved += counted.step(gate)
    g_att = lax.dot_general(
        after(g_ba, gate), weights[2], (((1,), (1,)), ((), ())), preferred_element_type=f32
    ).astype(bf16)
    attended = out_grad(att, after(g_ba, gate), width + 3 * half)
    gate = moved + [g_att]
    moved, gate = window(gate, ["up"])
    moved += counted.step(gate)
    gate = moved + back(0, gate)
    over_x, gate = window(gate, ["up"])
    over_x += counted.step(gate)
    attended = heads_grad(after(tokens, gate), [g3[0]], attended)
    own_att = lax.psum_scatter(attended, "shard", scatter_dimension=0, tiled=True)
    moved, gate = window([attended], ["down"])
    gate = moved + over_x + back(1, gate)
    first_up = after(first_up.reshape(2 * each, ff // 2), gate)
    last_up = at.along_y(first_up)
    counts = counted.total()
    count = jnp.maximum(counts[4, 0], 1.0)
    loss = counts[0, 0] / count
    scale = rows * at.reps * at.shards / count
    over_z, gate = window(gate, ["up"])
    sides = heads_grad(after(x_sorted, gate), [g3[1]], wide=PAIR)
    shorts = [
        jnp.concatenate(g_scale), grad_aa.reshape(-1), jnp.concatenate([su0, su1], axis=1).reshape(-1),
        jnp.concatenate([sg0, sg1], axis=1).reshape(-1), grad_am.reshape(-1),
    ]
    shorts = jnp.concatenate([s.reshape(at.shards, -1) for s in shorts], axis=1).astype(bf16)
    shorts = jnp.pad(shorts.reshape(groups, NC, each, per_row), ((0, 0), (0, 0), (0, 0), (0, PAIR - per_row)))
    sides = [
        lax.dynamic_update_slice(
            side, lax.dynamic_index_in_dim(shorts, which, axis=1, keepdims=False).reshape(-1, PAIR), (0, 3 * half)
        )
        for side, which in zip(sides, (1 - at.core, at.core))
    ]
    waiting["qkv1"] = Reduce(at, *sides)
    gate = list(sides) + [last_up]
    gate, _ = window(gate, ["qkv1"])
    gate, _ = window(gate, ["qkv1"])
    moved, sends = window(gate, ["qkv1"])
    last_down, _ = window(gate, ["down"])
    moved += last_down
    grad_x = input_grad(
        scale.reshape(1), after(gx_base, sends), [g3[0], g3[1]], [weights[0], weights[1]]
    )
    gate = moved + over_z + [grad_x]
    gate, _ = window(gate, ["qkv1", "up"])
    own_att = after(own_att, gate)
    last_att = at.along_y(own_att)
    window(gate, ["qkv1"])
    total = {name: chunk.total() * scale for name, chunk in waiting.items()}

    def whole(mine, other):
        return over_copies(at, mine.astype(f32) + other.astype(f32), 2) * scale

    attended = whole(own_att, last_att)
    q0, q1 = (jnp.split(v, 3, axis=1) for v in (attended[:, width:], total["qkv1"][:, : 3 * half]))
    shorts = total["qkv1"][:, 3 * half : 3 * half + per_row].reshape(-1)
    owned, place = [], 0
    for vector in vectors:
        owned.append(shorts[place : place + vector.shape[0]])
        place += vector.shape[0]
    own_qkv = jnp.concatenate([part for two in zip(q0, q1) for part in two], axis=1)
    first_up = whole(first_up, last_up)
    ups = [first_up[:each], total["up"][:each], first_up[each:], total["up"][each:]]
    own_up = jnp.concatenate(ups, axis=1)
    return (output, loss, grad_x, own_qkv, attended[:, :width], own_up, total["down"], *owned)


def solution(mesh):
    return jax.shard_map(
        body,
        mesh=mesh,
        in_specs=(
            P(("rep", "shard"), None),
            P(("rep", "shard"), None),
            P(("rep", "shard")),
            P(("rep", "shard"), None),
            P(("rep", "shard"), None),
            P("shard", None),
            P("shard", None),
            P("shard", None),
            P("shard", None),
            P("shard"),
            P("shard"),
            P("shard"),
            P("shard"),
            P("shard"),
        ),
        out_specs=(
            P(("rep", "shard"), None),
            P(),
            P(("rep", "shard"), None),
            P("shard", None),
            P("shard", None),
            P("shard", None),
            P("shard", None),
            P("shard"),
            P("shard"),
            P("shard"),
            P("shard"),
            P("shard"),
        ),
        check_vma=False,
    )
```
